256 devices in a mesh: dom: 256 (over y, z, x, core).
Axes of the slice: x: 4, y: 4, z: 8, core: 2. Of those that a mesh axis runs over, the one named last changes fastest.
Arguments:
- dofs: float32 [56, 9, 32768], P(None, None, 'dom'), may hold values from -6 to 6
- star: float32 [3, 9, 9, 32768], P(None, None, None, 'dom'), may hold values from -8 to 8
- flux_minus: float32 [4, 9, 9, 32768], P(None, None, None, 'dom'), may hold values from -0.4 to 0.4
- flux_plus: float32 [4, 9, 9, 32768], P(None, None, None, 'dom'), may hold values from -0.4 to 0.4
- cohesion: float32 [32768], P('dom'), may hold values from 0.5 to 4
- stiff: float32 [3, 56, 56], replicated, may hold values from -1 to 1
- face_proj: float32 [4, 21, 56], replicated, may hold values from -0.75 to 0.75
- lift: float32 [4, 56, 21], replicated, may hold values from -1.25 to 1.25
- rotate: float32 [3, 21, 21], replicated, may hold values from -1.25 to 1.25
- cluster: int32 [32768], P('dom'), may hold values from 0 to 1, as said below
- neighbor: int32 [4, 32768], P(None, 'dom'), may hold values from 0 to 256, as said below
- neigh_face: int32 [4, 32768], P(None, 'dom'), may hold values from 0 to 3, as said below
- orient: int32 [4, 32768], P(None, 'dom'), may hold values from 0 to 2, as said below
- send_elem: int32 [4, 8192], P(None, 'dom'), may hold values from 0 to 127, as said below
- send_face: int32 [4, 8192], P(None, 'dom'), may hold values from 0 to 3, as said below
Outputs:
- new_dofs: float32 [56, 9, 32768], P(None, None, 'dom')
The draws below stay inside these ranges and needn't reach their ends.
Inputs may be any that keep to these rules, and one draw needn't show every extreme that they name: `cluster`: each partition has at most 64 fine elements, and it has at most 96 together with the partition half the axis away; both bounds are reached in every draw. `neighbor`: values below 128 name an element of the same partition; 128 + b * 32 + s names slot s of the faces shared with the partition at offset -2, -1, 1, 2 for b = 0, 1, 2, 3, that is slot s of block 3 - b in that partition's send_elem and send_face; 256 marks the mesh's boundary. Every slot of an existing partition is named by exactly one face, and faces pair symmetrically. `neigh_face`: the neighbour's face across each face; for a shared slot it equals the slot's send_face; 0 on the boundary. `orient`: 0 on the boundary; a face pair's codes h and (3 - h) % 3. `send_elem`: block b holds, for slot s, the local element whose face the partition shares with the partition at offset -2, -1, 1, 2 for b = 0, 1, 2, 3. `send_face`: the face of that element in slot s of block b.
All inputs are finite; a program needn't handle non-finite values.
Results may differ from the reference program's by a relative error of at most 0.00024.
Values sent between devices are 32-bit elements; how exact they have to be, the bound alone decides.
No kernel may reach another device: no remote copies, remote signals or barrier semaphores. Data moves between devices by JAX's collectives and lax.ppermute only.
A program may use at most 128 MiB of HBM per device.

```python
import math
import jax
import jax.numpy as jnp
from jax import lax

BASIS = 56
FACE_BASIS = 21
QUANT = 9
ORDER = 6
RATE = 4
ELEM_DEV = 128
SLOTS = 32
FINE_CAP = 64
PAIR_CAP = 96
ELEMENTS = 32768
N_DOM = 256


def mesh_tables(key):
    devices = ELEMENTS // ELEM_DEV
    local_faces = 4 * ELEM_DEV
    crossing = 4 * SLOTS
    boundary = ELEM_DEV + 4 * SLOTS
    base = jax.random.fold_in(key, 4411)
    perm_key, cross_key, inner_key = jax.random.split(base, 3)
    orders = jax.vmap(lambda single: jax.random.permutation(single, local_faces))(jax.random.split(perm_key, devices)).astype(jnp.int32)
    cross_turn = jax.random.randint(cross_key, (devices, 2, SLOTS), 0, 3, dtype=jnp.int32)
    inner_pairs = (local_faces - crossing) // 2
    inner_turn = jax.random.randint(inner_key, (devices, inner_pairs), 0, 3, dtype=jnp.int32)
    partner = jnp.full((devices, local_faces), boundary, jnp.int32)
    across = jnp.zeros((devices, local_faces), jnp.int32)
    turning = jnp.zeros((devices, local_faces), jnp.int32)
    device_rows = jnp.arange(devices, dtype=jnp.int32)[:, None]
    first_half = orders[:, crossing::2]
    second_half = orders[:, crossing + 1::2]
    partner = partner.at[device_rows, first_half].set(second_half // 4)
    partner = partner.at[device_rows, second_half].set(first_half // 4)
    across = across.at[device_rows, first_half].set(second_half % 4)
    across = across.at[device_rows, second_half].set(first_half % 4)
    turning = turning.at[device_rows, first_half].set(inner_turn)
    turning = turning.at[device_rows, second_half].set((3 - inner_turn) % 3)
    slot_ids = jnp.arange(SLOTS, dtype=jnp.int32)[None, :]
    for step_size in (1, 2):
        upper = 1 + step_size
        lower = 2 - step_size
        upward = orders[:, upper * SLOTS:(upper + 1) * SLOTS]
        downward = orders[:, lower * SLOTS:(lower + 1) * SLOTS]
        turn_up = cross_turn[:, step_size - 1, :]
        has_up = device_rows + step_size < devices
        has_down = device_rows - step_size >= 0
        from_up = jnp.roll(downward, -step_size, axis=0)
        from_down = jnp.roll(upward, step_size, axis=0)
        turn_down = jnp.roll(turn_up, step_size, axis=0)
        partner = partner.at[device_rows, upward].set(jnp.where(has_up, ELEM_DEV + upper * SLOTS + slot_ids, boundary))
        across = across.at[device_rows, upward].set(jnp.where(has_up, from_up % 4, 0))
        turning = turning.at[device_rows, upward].set(jnp.where(has_up, turn_up, 0))
        partner = partner.at[device_rows, downward].set(jnp.where(has_down, ELEM_DEV + lower * SLOTS + slot_ids, boundary))
        across = across.at[device_rows, downward].set(jnp.where(has_down, from_down % 4, 0))
        turning = turning.at[device_rows, downward].set(jnp.where(has_down, (3 - turn_down) % 3, 0))
    sending = orders[:, :crossing].reshape(devices, 4, SLOTS)
    return (partner, across, turning, sending // 4, sending % 4)


def to_faces(table):
    return jnp.transpose(table.reshape(-1, ELEM_DEV, 4), (2, 0, 1)).reshape(4, -1).astype(jnp.int32)


def to_slots(table):
    return jnp.transpose(table, (1, 0, 2)).reshape(4, -1).astype(jnp.int32)


def draw_neighbor(key, part):
    return to_faces(mesh_tables(key)[0])


def draw_neigh_face(key, part):
    return to_faces(mesh_tables(key)[1])


def draw_orient(key, part):
    return to_faces(mesh_tables(key)[2])


def draw_send_elem(key, part):
    return to_slots(mesh_tables(key)[3])


def draw_send_face(key, part):
    return to_slots(mesh_tables(key)[4])


def draw_cluster(key, part):
    devices = ELEMENTS // ELEM_DEV
    pair_count = devices // 2
    base = jax.random.fold_in(key, 9127)
    total_key, spare_key, flip_key, rank_key = jax.random.split(base, 4)
    totals = jax.random.randint(total_key, (pair_count,), ELEM_DEV // 8, PAIR_CAP + 1, dtype=jnp.int32)
    totals = totals.at[0].set(PAIR_CAP)
    spare = jax.random.randint(spare_key, (pair_count,), 0, ELEM_DEV, dtype=jnp.int32) % (totals // 4 + 1)
    busy = jnp.minimum(FINE_CAP, totals - spare)
    quiet = totals - busy
    flipped = jax.random.randint(flip_key, (pair_count,), 0, 2, dtype=jnp.int32)
    lower_count = jnp.where(flipped == 1, busy, quiet)
    upper_count = jnp.where(flipped == 1, quiet, busy)
    counts = jnp.concatenate([lower_count, upper_count])
    ranks = jax.vmap(lambda single: jax.random.permutation(single, ELEM_DEV))(jax.random.split(rank_key, devices))
    return (ranks < counts[:, None]).astype(jnp.int32).reshape(-1)


def draw_star(key, part):
    labels = draw_cluster(key, part)
    star_key = jax.random.fold_in(key, 5233)
    raw = jax.random.normal(star_key, (3, QUANT, QUANT, ELEMENTS), jnp.float32)
    values = jnp.clip(0.35 * raw, -2.0, 2.0)
    factor = jnp.where(labels == 1, 4.0, 1.0).astype(jnp.float32)
    return (values * factor[None, None, None, :]).astype(jnp.float32)


def levels(stream_key, shape, cuts, low, high):
    loudness = 1.0
    for position, shards_of in cuts:
        draws = jax.random.uniform(jax.random.fold_in(jax.random.fold_in(stream_key, 6), position), (shards_of,), jnp.float32, low / len(cuts), high / len(cuts))
        loudness = loudness * jnp.repeat(jnp.exp(draws), shape[position] // shards_of).reshape((-1,) + (1,) * (len(shape) - 1 - position))
    return loudness


def gaussian(own_key, shape, spread, most, shards=(), kind=jnp.bfloat16):
    values = spread * jax.random.normal(own_key, shape, jnp.float32)
    if shards:
        values = values * levels(own_key, shape, shards, -0.22, 0.18)
    return jnp.clip(values, -most, most).astype(kind)


def setup_inputs(seed: int = 0) -> dict:
    keys = jax.random.split(jax.random.key(seed), 16)
    return {
        "dofs": gaussian(keys[0], (BASIS, QUANT, ELEMENTS), 1.0, 6.0, ((2, 256),), jnp.float32),
        "star": draw_star(jax.random.fold_in(keys[15], 71), 0),
        "flux_minus": gaussian(keys[2], (4, QUANT, QUANT, ELEMENTS), 0.05, 0.4, ((3, 256),), jnp.float32),
        "flux_plus": gaussian(keys[3], (4, QUANT, QUANT, ELEMENTS), 0.05, 0.4, ((3, 256),), jnp.float32),
        "cohesion": jnp.clip(jnp.exp(math.log(4.0) - 2.0794415 * jax.random.uniform(keys[4], (ELEMENTS,), jnp.float32) ** levels(keys[4], (ELEMENTS,), ((0, 256),), -0.2, 0.2)), 0.5, 4.0),
        "stiff": gaussian(keys[5], (3, BASIS, BASIS), (BASIS // 2) ** -0.5, 1.0, (), jnp.float32),
        "face_proj": gaussian(keys[6], (4, FACE_BASIS, BASIS), BASIS ** -0.5, 0.75, (), jnp.float32),
        "lift": gaussian(keys[7], (4, BASIS, FACE_BASIS), FACE_BASIS ** -0.5, 1.25, (), jnp.float32),
        "rotate": gaussian(keys[8], (3, FACE_BASIS, FACE_BASIS), FACE_BASIS ** -0.5, 1.25, (), jnp.float32),
        "cluster": draw_cluster(jax.random.fold_in(keys[15], 71), 0),
        "neighbor": draw_neighbor(jax.random.fold_in(keys[15], 71), 0),
        "neigh_face": draw_neigh_face(jax.random.fold_in(keys[15], 71), 0),
        "orient": draw_orient(jax.random.fold_in(keys[15], 71), 0),
        "send_elem": draw_send_elem(jax.random.fold_in(keys[15], 71), 0),
        "send_face": draw_send_face(jax.random.fold_in(keys[15], 71), 0),
    }


PRECISE = lax.Precision.HIGHEST

def prepare(stiff, star):
    skew = 0.5 * (stiff - jnp.transpose(stiff, (0, 2, 1)))
    sym = 0.5 * (star + jnp.transpose(star, (0, 2, 1, 3)))
    return (skew, sym)

def operator_left(skew, transposed):
    basis_size = skew.shape[1]
    order_axes = (2, 0, 1) if transposed else (1, 0, 2)
    return jnp.transpose(skew, order_axes).reshape(basis_size, 3 * basis_size)

def star_apply(matrices, values):
    running = jnp.expand_dims(matrices[..., 0, :], -3) * values[..., 0:1, :]
    for column in range(1, values.shape[-2]):
        running = running + jnp.expand_dims(matrices[..., column, :], -3) * values[..., column:column + 1, :]
    return running

def apply_operator(values, left_matrix, sym):
    stacked = jnp.stack([star_apply(sym[direction], values) for direction in range(3)])
    product = jnp.dot(left_matrix, stacked.reshape(left_matrix.shape[1], -1), precision=PRECISE)
    return product.reshape(values.shape)

def derivatives(values, left_matrix, sym):
    series = [values]
    for term in range(ORDER - 1):
        series.append(-apply_operator(series[-1], left_matrix, sym))
    return series

def interval_weights(begin_time, end_time):
    return [(end_time ** (term + 1) - begin_time ** (term + 1)) / math.factorial(term + 1) for term in range(ORDER)]

def integrate(series, weights):
    running = weights[0] * series[0]
    for term in range(1, ORDER):
        running = running + weights[term] * series[term]
    return running

def traces(values, face_proj):
    face_count, fbasis, basis_size = face_proj.shape
    product = jnp.dot(face_proj.reshape(face_count * fbasis, basis_size), values.reshape(basis_size, -1), precision=PRECISE)
    return product.reshape(face_count, fbasis, values.shape[1], values.shape[2])

def lift_apply(face_values, lift):
    face_count, basis_size, fbasis = lift.shape
    left_matrix = jnp.transpose(lift, (1, 0, 2)).reshape(basis_size, face_count * fbasis)
    product = jnp.dot(left_matrix, face_values.reshape(face_count * fbasis, -1), precision=PRECISE)
    return product.reshape(basis_size, face_values.shape[2], face_values.shape[3])

def rotate_apply(face_values, orient, rotate):
    turned = jnp.einsum('kij,fjqm->kfiqm', rotate, face_values, precision=PRECISE)
    rotation = orient[:, None, None, :]
    return jnp.where(rotation == 0, turned[0], jnp.where(rotation == 1, turned[1], turned[2]))

def plastic(values, cohesion):
    average = values[0]
    mean_stress = (average[0] + average[1] + average[2]) / 3.0
    dev_xx = average[0] - mean_stress
    dev_yy = average[1] - mean_stress
    dev_zz = average[2] - mean_stress
    second = 0.5 * (dev_xx * dev_xx + dev_yy * dev_yy + dev_zz * dev_zz) + average[3] * average[3] + average[4] * average[4] + average[5] * average[5]
    factor = cohesion / jnp.maximum(jnp.sqrt(second), cohesion)
    pressure = (values[:, 0] + values[:, 1] + values[:, 2]) / 3.0
    normal = pressure[:, None, :] + factor * (values[:, 0:3, :] - pressure[:, None, :])
    shear_part = factor * values[:, 3:6, :]
    return jnp.concatenate([normal, shear_part, values[:, 6:, :]], axis=1)

def update(values, predictor, own_faces, remote_faces, orient, back_left, sym, flux_minus, flux_plus, cohesion, lift, rotate):
    volume_term = apply_operator(predictor, back_left, sym)
    local_term = lift_apply(star_apply(flux_minus, own_faces), lift)
    remote_term = lift_apply(star_apply(flux_plus, rotate_apply(remote_faces, orient, rotate)), lift)
    return plastic(values + volume_term - local_term - remote_term, cohesion)

def flatten_faces(face_values):
    face_count, fbasis, quantities, columns = face_values.shape
    return jnp.transpose(face_values, (0, 3, 1, 2)).reshape(face_count * columns, fbasis * quantities)

def lookup(face_values, face_ids, targets, usable):
    face_count, fbasis, quantities, columns = face_values.shape
    flattened = flatten_faces(face_values)
    picked = jnp.take(flattened, (face_ids * columns + targets).reshape(-1), axis=0)
    picked = jnp.where(usable.reshape(-1)[:, None], picked, 0.0)
    return jnp.transpose(picked.reshape(face_count, -1, fbasis, quantities), (0, 2, 3, 1))

def reference(dofs, star, flux_minus, flux_plus, cohesion, stiff, face_proj, lift, rotate, cluster, neighbor, neigh_face, orient, send_elem, send_face):
    skew, sym = prepare(stiff, star)
    forward_left = operator_left(skew, False)
    back_left = operator_left(skew, True)
    elements = dofs.shape[2]
    device_of = jnp.arange(elements, dtype=jnp.int32) // ELEM_DEV
    ghost_offset = neighbor - ELEM_DEV
    is_local = neighbor < ELEM_DEV
    is_ghost = (ghost_offset >= 0) & (ghost_offset < 4 * SLOTS)
    usable = is_local | is_ghost
    block = jnp.clip(ghost_offset // SLOTS, 0, 3).astype(jnp.int32)
    slot_id = jnp.clip(ghost_offset % SLOTS, 0, SLOTS - 1).astype(jnp.int32)
    offset_table = jnp.array([-2, -1, 1, 2], dtype=jnp.int32)
    source = jnp.clip(device_of[None, :] + offset_table[block], 0, N_DOM - 1).astype(jnp.int32)
    sender_elem = send_elem[3 - block, source * SLOTS + slot_id]
    sender_face = send_face[3 - block, source * SLOTS + slot_id]
    local_target = device_of[None, :] * ELEM_DEV + jnp.clip(neighbor, 0, ELEM_DEV - 1)
    targets = jnp.where(is_local, local_target, source * ELEM_DEV + sender_elem)
    targets = jnp.where(usable, targets, 0).astype(jnp.int32)
    face_ids = jnp.where(is_local, neigh_face, sender_face).astype(jnp.int32)
    fine = (cluster == 1)[None, None, :]
    series = derivatives(dofs, forward_left, sym)
    full = integrate(series, interval_weights(0.0, 1.0))
    pieces = [integrate(series, interval_weights(substep / RATE, (substep + 1) / RATE)) for substep in range(RATE)]
    fine_weights = interval_weights(0.0, 1.0 / RATE)
    state_fine = dofs
    accumulated = pieces[0]
    for substep in range(RATE):
        if substep == 0:
            predictor = pieces[0]
        else:
            own_pred = integrate(derivatives(state_fine, forward_left, sym), fine_weights)
            predictor = jnp.where(fine, own_pred, pieces[substep])
            accumulated = accumulated + predictor
        face_values = traces(predictor, face_proj)
        remote = lookup(face_values, face_ids, targets, usable)
        stepped = update(state_fine, predictor, face_values, remote, orient, back_left, sym, flux_minus, flux_plus, cohesion, lift, rotate)
        state_fine = jnp.where(fine, stepped, state_fine)
    remote_all = lookup(traces(accumulated, face_proj), face_ids, targets, usable)
    coarse = update(dofs, full, traces(full, face_proj), remote_all, orient, back_left, sym, flux_minus, flux_plus, cohesion, lift, rotate)
    return jnp.where(fine, state_fine, coarse)
```

```python
import functools

import jax
import jax.numpy as jnp
from jax import lax
from jax.experimental import pallas as pl
from jax.experimental.pallas import tpu as pltpu
from jax.sharding import PartitionSpec as P

ORDER = 6
RATE = 4
F32 = jnp.float32
BF16 = jnp.bfloat16
NB = 56
NQ = 9
FR = 24
FA = 4 * FR
LN = 128
PK = 56


def dot(a, b):
    return jnp.dot(a, b, preferred_element_type=F32)


def exact(a, b):
    return jnp.dot(a, b, preferred_element_type=F32, precision=lax.Precision.HIGHEST)


def split(x):
    hi = x.astype(BF16)
    return hi, (x - hi.astype(F32)).astype(BF16)


def two_rows(w, pad):
    if w.shape[0] < pad:
        w = jnp.concatenate([w, jnp.zeros((pad - w.shape[0], w.shape[1]), F32)], axis=0)
    return jnp.concatenate(split(w), axis=0)


def times(w2, rhs, rows):
    half = w2.shape[0] // 2
    hi, lo = split(rhs)
    both = dot(w2, hi)
    return both[:rows] + both[half:half + rows] + dot(w2[:half], lo)[:rows]


def star_rows(s_ref, group, values):
    total = s_ref[group, 0:1, :] * values(0)
    for p in range(1, NQ):
        total = total + s_ref[group, p:p + 1, :] * values(p)
    return total


def operator(x_ref, s_ref, w2):
    out = []
    for q in range(NQ):
        stacked = jnp.concatenate(
            [star_rows(s_ref, c * NQ + q, lambda p: x_ref[p]) for c in range(3)], axis=0)
        out.append(times(w2, stacked, NB))
    return out


def traces(x_ref, p2, t_ref):
    for q in range(NQ):
        t_ref[q] = times(p2, x_ref[q], FA)


def lanes(shape):
    return lax.broadcasted_iota(jnp.int32, shape, len(shape) - 1)


def pick(rows, index):
    return jnp.take_along_axis(rows, index, axis=1, mode="promise_in_bounds")


def send(t_ref, se_ref, sf_ref, out_refs):
    elem = jnp.broadcast_to(se_ref[...], (FR, LN))
    face = jnp.broadcast_to(sf_ref[...], (FR, LN))
    rows = []
    for q in range(NQ):
        got = pick(t_ref[q, 0:FR], elem)
        for f in range(1, 4):
            got = jnp.where(face == f, pick(t_ref[q, f * FR:(f + 1) * FR], elem), got)
        rows.append(got)
    rows.append(jnp.zeros((4 * PK - NQ * FR, LN), F32))
    table = jnp.concatenate(rows, axis=0)
    group = lanes((PK, LN)) // 32
    for k in range(4):
        message = None
        for g in range(4):
            part = table[g * PK:(g + 1) * PK]
            if g != k:
                part = pltpu.roll(part, ((g - k) * 32) % LN, 1)
            message = part if message is None else jnp.where(group == g, part, message)
        out_refs[k][...] = message


def unpack(in_refs):
    group = lanes((PK, LN)) // 32
    parts = []
    for g in range(4):
        rows = None
        for k in range(4):
            part = in_refs[k][...]
            if g != k:
                part = pltpu.roll(part, ((k - g) * 32) % LN, 1)
            rows = part if rows is None else jnp.where(group == k, part, rows)
        parts.append(rows)
    return jnp.concatenate(parts, axis=0)


def local_pick(t_ref, nb_ref, nf_ref, out_ref):
    for f in range(4):
        where = jnp.broadcast_to(nb_ref[f:f + 1, :], (FR, LN))
        face = jnp.broadcast_to(nf_ref[f:f + 1, :], (FR, LN))
        elem = jnp.minimum(where, LN - 1)
        face = jnp.where(where < LN, face, 4)
        for q in range(NQ):
            got = jnp.zeros((FR, LN), F32)
            for g in range(4):
                got = jnp.where(face == g, pick(t_ref[q, g * FR:(g + 1) * FR], elem), got)
            out_ref[q, f * FR:(f + 1) * FR] = got


def ghost_pick(table, nb_ref, local_ref, out_ref):
    for f in range(4):
        where = jnp.broadcast_to(nb_ref[f:f + 1, :], (FR, LN))
        slot = jnp.clip(where - LN, 0, LN - 1)
        ghost = (where >= LN) & (where < 2 * LN)
        for q in range(NQ):
            got = pick(table[q * FR:(q + 1) * FR], slot)
            out_ref[q, f * FR:(f + 1) * FR] = jnp.where(
                ghost, got, local_ref[q, f * FR:(f + 1) * FR])


def flux_rows(f_ref, q, t_ref):
    return jnp.concatenate(
        [star_rows(f_ref, f * NQ + q, lambda p: t_ref[p, f * FR:(f + 1) * FR]) for f in range(4)],
        axis=0)


def own_term(f_ref, t_ref, l2, q):
    return times(l2, flux_rows(f_ref, q, t_ref), NB)


def orient_masks(or_ref):
    codes = jnp.concatenate(
        [jnp.broadcast_to(or_ref[f:f + 1, :], (FR, LN)) for f in range(4)], axis=0)
    return [(codes == k).astype(F32).astype(BF16) for k in range(3)]


def plastic(u_ref, cohesion):
    s = [u_ref[q, 0:1, :] for q in range(6)]
    mean = (s[0] + s[1] + s[2]) / 3.0
    dx, dy, dz = s[0] - mean, s[1] - mean, s[2] - mean
    second = 0.5 * (dx * dx + dy * dy + dz * dz) + s[3] * s[3] + s[4] * s[4] + s[5] * s[5]
    factor = cohesion / jnp.maximum(jnp.sqrt(second), cohesion)
    pressure = (u_ref[0] + u_ref[1] + u_ref[2]) / 3.0
    out = [pressure + factor * (u_ref[i] - pressure) for i in range(3)]
    out += [factor * u_ref[i] for i in range(3, 6)]
    return out + [u_ref[i] for i in range(6, NQ)]


def place(width, offset, rows):
    r = lax.broadcasted_iota(jnp.int32, (rows, width), 0)
    return (lanes((rows, width)) == r + offset).astype(F32)


def first_kernel(dofs, star, stiff, proj, se, sf, s_out, w2_out, p2_out, x_out, pieces, t_out,
                 m0, m1, m2, m3, series):
    for c in range(3):
        for q in range(NQ):
            s_out[c * NQ + q] = 0.5 * (star[c, q] + star[c, :, q, :])
    w = None
    for c in range(3):
        minus = 0.5 * (jnp.transpose(stiff[c]) - stiff[c])
        part = exact(minus, place(3 * NB, c * NB, NB))
        w = part if w is None else w + part
    w2_out[...] = two_rows(w, 64)
    faces = []
    for f in range(4):
        faces += [proj[f], jnp.zeros((FR - proj.shape[1], NB), F32)]
    p2_out[...] = two_rows(jnp.concatenate(faces, axis=0), FA)
    for q in range(NQ):
        x = dofs[:, q, :]
        x_out[q] = x
        series[q] = x
        for s in range(RATE):
            pieces[s, q] = x * (1.0 / RATE)

    def step(k, powers):
        kf = k.astype(F32)
        powers = [powers[j] * ((j + 1) / RATE / (kf + 2.0)) for j in range(RATE)]
        rows = operator(series, s_out, w2_out[...])
        for q in range(NQ):
            series[q] = rows[q]
            for s in range(RATE):
                weight = powers[s] - powers[s - 1] if s else powers[0]
                pieces[s, q] += weight * rows[q]
        return powers

    lax.fori_loop(0, ORDER - 1, step, [jnp.float32((j + 1) / RATE) for j in range(RATE)])
    traces(pieces.at[0], p2_out[...], t_out)
    send(t_out, se, sf, (m0, m1, m2, m3))


def lift_kernel(x_ref, s_ref, w2, p2, pieces, fm_ref, lift, rotate, l2_out, lr2_out, u_out,
                full, t_full):
    own, turned = None, [None] * 3
    for f in range(4):
        spot = place(FA, f * FR, lift.shape[2])
        part = exact(lift[f], spot)
        own = part if own is None else own + part
        for k in range(3):
            part = exact(exact(lift[f], rotate[k]), spot)
            turned[k] = part if turned[k] is None else turned[k] + part
    l2_out[...] = two_rows(own, 64)
    for k in range(3):
        lr2_out[k] = two_rows(turned[k], 64)
    for q in range(NQ):
        full[q] = pieces[0, q] + pieces[1, q] + pieces[2, q] + pieces[3, q]
    traces(full, p2[...], t_full)

    rows = operator(full, s_ref, w2[...])
    for q in range(NQ):
        u_out[q] = x_ref[q] + rows[q] - own_term(fm_ref, t_full, l2_out[...], q)


def local_kernel(q_ref, pred, t_ref, s_ref, w2, fm_ref, l2, nb_ref, nf_ref, u_out, n_out):
    rows = operator(pred, s_ref, w2[...])
    for q in range(NQ):
        u_out[q] = q_ref[q] + rows[q] - own_term(fm_ref, t_ref, l2[...], q)
    local_pick(t_ref, nb_ref, nf_ref, n_out)


def join_kernel(last, *refs):
    (g0, g1, g2, g3, q_ref, u_ref, nl_ref, nacc_ref, fp_ref, lr2, nb_ref, or_ref, coh, fine_ref,
     s_ref, w2, p2, piece, se, sf) = refs[:20]
    table = unpack((g0, g1, g2, g3))
    masks = orient_masks(or_ref)
    fine = fine_ref[...] == 1
    if last:
        uc_ref, out, n_ref, work = refs[20:]
    else:
        q_out, n_out, pred, t_out, m0, m1, m2, m3, n_ref, work, series = refs[20:]

    def face_terms(values):
        for q in range(NQ):
            hi, lo = split(flux_rows(fp_ref, q, n_ref))
            sub = None
            for k in range(3):
                w = lr2[k]
                both = dot(w, hi * masks[k])
                part = both[:NB] + both[64:64 + NB] + dot(w[:64], lo * masks[k])[:NB]
                sub = part if sub is None else sub + part
            work[q] = values[q] - sub

    ghost_pick(table, nb_ref, nl_ref, n_ref)
    face_terms(u_ref)
    after = plastic(work, coh[...])
    if last:
        for q in range(NQ):
            out[:, q, :] = after[q]
        for q in range(NQ):
            n_ref[q] += nacc_ref[q]
        face_terms(uc_ref)
        after = plastic(work, coh[...])
        for q in range(NQ):
            out[:, q, :] = jnp.where(fine, out[:, q, :], after[q])
        return
    for q in range(NQ):
        n_out[q] = nacc_ref[q] + n_ref[q] if nacc_ref is not None else n_ref[q]
        x = jnp.where(fine, after[q], q_ref[q])
        q_out[q] = x
        series[q] = x
        pred[q] = x * (1.0 / RATE)

    def step(k, weight):
        weight = weight * (1.0 / RATE / (k.astype(F32) + 2.0))
        rows = operator(series, s_ref, w2[...])
        for q in range(NQ):
            series[q] = rows[q]
            pred[q] += weight * rows[q]
        return weight

    lax.fori_loop(0, ORDER - 1, step, jnp.float32(1.0 / RATE))
    for q in range(NQ):
        pred[q] = jnp.where(fine, pred[q], piece[0, q])
    traces(pred, p2[...], t_out)
    send(t_out, se, sf, (m0, m1, m2, m3))


BIG = (NQ, NB, LN)
TAB = (NQ, FA, LN)
MSG = (PK, LN)


def call(kernel, name, outs, scratch, args, flops=50_000_000):
    return pl.pallas_call(
        kernel,
        name=name,
        out_shape=[jax.ShapeDtypeStruct(s, d) for s, d in outs],
        in_specs=[pl.BlockSpec(memory_space=pltpu.VMEM)] * len(args),
        out_specs=[pl.BlockSpec(memory_space=pltpu.VMEM)] * len(outs),
        scratch_shapes=[pltpu.VMEM(s, d) for s, d in scratch],
        compiler_params=pltpu.CompilerParams(vmem_limit_bytes=24 << 20),
        cost_estimate=pl.CostEstimate(flops=flops, bytes_accessed=4 << 20, transcendentals=0),
    )(*args)


def partners(devices):
    def pairing(step, start, ends):
        pairs = []
        for i in range(devices):
            j = i - start
            t = start + (j ^ step) if j >= 0 else -1
            if t < start or t >= devices:
                t = ends(i)
            pairs.append((i, t))
        return pairs
    return (
        pairing(1, 0, lambda i: i),
        pairing(1, 1, lambda i: devices - 1 - i),
        pairing(2, 0, lambda i: i),
        pairing(2, 2, lambda i: i ^ 1),
    )


def shards(dofs, star, flux_minus, flux_plus, cohesion, stiff, face_proj, lift, rotate, cluster,
           neighbor, neigh_face, orient, send_elem, send_face):
    devices = lax.axis_size("dom")
    me = lax.axis_index("dom")
    pairings = partners(devices)
    one_up = me % 2 == 0
    two_up = me % 4 < 2
    slots = send_elem.shape[1]

    def reorder(table):
        b0, b1, b2, b3 = table[0], table[1], table[2], table[3]
        return jnp.concatenate([
            jnp.where(one_up, b2, b1), jnp.where(one_up, b1, b2),
            jnp.where(two_up, b3, b0), jnp.where(two_up, b0, b3)]).reshape(1, 4 * slots)

    se, sf = reorder(send_elem), reorder(send_face)
    ghost = neighbor - LN
    block, slot = ghost // slots, ghost % slots
    one = (block == 1) | (block == 2)
    place_of = jnp.where(
        one,
        jnp.where((block == 2) == one_up, 0, 1),
        jnp.where((block == 3) == two_up, 2, 3))
    nb = jnp.where((ghost >= 0) & (ghost < 4 * slots), LN + place_of * slots + slot, neighbor)
    fm = flux_minus.reshape(4 * NQ, NQ, LN)
    fp = flux_plus.reshape(4 * NQ, NQ, LN)
    coh = cohesion.reshape(1, LN)
    fine = cluster.reshape(1, LN)

    def exchange(messages):
        got = [None] * 4
        for k in (2, 3, 1, 0):
            got[k] = lax.ppermute(messages[k], "dom", pairings[k])
        return got

    outs = call(
        first_kernel, "first",
        [((27, NQ, LN), F32), ((128, 3 * NB), BF16), ((2 * FA, NB), BF16), (BIG, F32),
         ((RATE,) + BIG, F32), (TAB, F32)] + [(MSG, F32)] * 4,
        [(BIG, F32)],
        [dofs, star, stiff, face_proj, se, sf])
    s_mat, w2, p2, state, pieces, table = outs[:6]
    got = exchange(outs[6:])
    l2, lr2, coarse = call(
        lift_kernel, "coarse_own",
        [((128, FA), BF16), ((3, 128, FA), BF16), (BIG, F32)],
        [(BIG, F32), (TAB, F32)],
        [state, s_mat, w2, p2, pieces, fm, lift, rotate])
    total = None
    pred = pieces[0]
    for sub in range(RATE):
        u, near = call(
            local_kernel, "local", [(BIG, F32), (TAB, F32)], [],
            [state, pred, table, s_mat, w2, fm, l2, nb, neigh_face])
        last = sub == RATE - 1
        common = [*got, state, u, near, total if total is not None else near, fp, lr2, nb, orient,
                  coh, fine, s_mat, w2, p2]
        if last:
            return call(
                functools.partial(join_kernel, True), "last",
                [((NB, NQ, LN), F32)],
                [(TAB, F32), (BIG, F32)],
                common + [pieces[3:4], se, sf, coarse])[0]
        first = total is None

        def kernel(*refs, first=first):
            refs = list(refs)
            if first:
                refs[7] = None
            join_kernel(False, *refs)

        outs = call(
            kernel, "join",
            [(BIG, F32), (TAB, F32), (BIG, F32), (TAB, F32)] + [(MSG, F32)] * 4,
            [(TAB, F32), (BIG, F32), (BIG, F32)],
            common + [pieces[sub + 1:sub + 2], se, sf])
        state, total, pred, table = outs[:4]
        got = exchange(outs[4:])


def solution(mesh):
    placed = (
        P(None, None, "dom"),
        P(None, None, None, "dom"),
        P(None, None, None, "dom"),
        P(None, None, None, "dom"),
        P("dom"),
        P(),
        P(),
        P(),
        P(),
        P("dom"),
        P(None, "dom"),
        P(None, "dom"),
        P(None, "dom"),
        P(None, "dom"),
        P(None, "dom"),
    )
    return jax.shard_map(
        shards, mesh=mesh, in_specs=placed, out_specs=P(None, None, "dom"), check_vma=False)
```

```python
import functools
import math

import jax
import jax.numpy as jnp
from jax import lax
from jax.experimental import pallas as pl
from jax.experimental.pallas import tpu as pltpu
from jax.sharding import PartitionSpec as P

ORDER = 6
RATE = 4
F32 = jnp.float32
BF16 = jnp.bfloat16
NB = 56
NQ = 9
FR = 24
FA = 4 * FR
LN = 128
PK = 56


def dot(a, b):
    return jnp.dot(a, b, preferred_element_type=F32)


def exact(a, b):
    return jnp.dot(a, b, preferred_element_type=F32, precision=lax.Precision.HIGHEST)


def split(x):
    hi = x.astype(BF16)
    return hi, (x - hi.astype(F32)).astype(BF16)


def two_rows(w, pad):
    if w.shape[0] < pad:
        w = jnp.concatenate([w, jnp.zeros((pad - w.shape[0], w.shape[1]), F32)], axis=0)
    return jnp.concatenate(split(w), axis=0)


def times(w2, rhs, rows):
    half = w2.shape[0] // 2
    hi, lo = split(rhs)
    both = dot(w2, hi)
    return both[:rows] + both[half:half + rows] + dot(w2[:half], lo)[:rows]


def star_rows(s_ref, q, which, values):
    total = s_ref[q, 0, which:which + 1, :] * values(0)
    for p in range(1, NQ):
        total = total + s_ref[q, p, which:which + 1, :] * values(p)
    return total


def operator(x_ref, s_ref, w2):
    out = []
    for q in range(NQ):
        stacked = jnp.concatenate(
            [star_rows(s_ref, q, c, lambda p: x_ref[p]) for c in range(3)], axis=0)
        out.append(times(w2, stacked, NB))
    return out


def traces(x_ref, p2, t_ref):
    for q in range(NQ):
        t_ref[q] = times(p2, x_ref[q], FA)


def lanes(shape):
    return lax.broadcasted_iota(jnp.int32, shape, len(shape) - 1)


def pick(rows, index):
    return jnp.take_along_axis(rows, index, axis=1, mode="promise_in_bounds")


def send(t_ref, se_ref, sf_ref, out_refs):
    elem = jnp.broadcast_to(se_ref[...], (FR, LN))
    face = jnp.broadcast_to(sf_ref[...], (FR, LN))
    rows = []
    for q in range(NQ):
        got = pick(t_ref[q, 0:FR], elem)
        for f in range(1, 4):
            got = jnp.where(face == f, pick(t_ref[q, f * FR:(f + 1) * FR], elem), got)
        rows.append(got)
    rows.append(jnp.zeros((4 * PK - NQ * FR, LN), F32))
    table = jnp.concatenate(rows, axis=0)
    group = lanes((PK, LN)) // 32
    for k in range(4):
        message = None
        for g in range(4):
            part = table[g * PK:(g + 1) * PK]
            if g != k:
                part = pltpu.roll(part, ((g - k) * 32) % LN, 1)
            message = part if message is None else jnp.where(group == g, part, message)
        out_refs[k][...] = message


def unpack(in_refs):
    group = lanes((PK, LN)) // 32
    parts = []
    for g in range(4):
        rows = None
        for k in range(4):
            part = in_refs[k][...]
            if g != k:
                part = pltpu.roll(part, ((k - g) * 32) % LN, 1)
            rows = part if rows is None else jnp.where(group == k, part, rows)
        parts.append(rows)
    return jnp.concatenate(parts, axis=0)


def local_pick(t_ref, nb_ref, nf_ref, out_ref):
    for f in range(4):
        where = jnp.broadcast_to(nb_ref[f:f + 1, :], (FR, LN))
        face = jnp.broadcast_to(nf_ref[f:f + 1, :], (FR, LN))
        elem = jnp.minimum(where, LN - 1)
        face = jnp.where(where < LN, face, 4)
        for q in range(NQ):
            got = jnp.zeros((FR, LN), F32)
            for g in range(4):
                got = jnp.where(face == g, pick(t_ref[q, g * FR:(g + 1) * FR], elem), got)
            out_ref[q, f * FR:(f + 1) * FR] = got


def ghost_pick(table, nb_ref, local_ref, out_ref):
    for f in range(4):
        where = jnp.broadcast_to(nb_ref[f:f + 1, :], (FR, LN))
        slot = jnp.clip(where - LN, 0, LN - 1)
        ghost = (where >= LN) & (where < 2 * LN)
        for q in range(NQ):
            got = pick(table[q * FR:(q + 1) * FR], slot)
            out_ref[q, f * FR:(f + 1) * FR] = jnp.where(
                ghost, got, local_ref[q, f * FR:(f + 1) * FR])


def flux_rows(f_ref, q, t_ref):
    return jnp.concatenate(
        [star_rows(f_ref, q, f, lambda p: t_ref[p, f * FR:(f + 1) * FR]) for f in range(4)],
        axis=0)


def own_term(f_ref, t_ref, l2, q):
    return times(l2, flux_rows(f_ref, q, t_ref), NB)


def orient_masks(or_ref):
    codes = jnp.concatenate(
        [jnp.broadcast_to(or_ref[f:f + 1, :], (FR, LN)) for f in range(4)], axis=0)
    return [(codes == k).astype(F32).astype(BF16) for k in range(3)]


def plastic(u_ref, cohesion):
    s = [u_ref[q, 0:1, :] for q in range(6)]
    mean = (s[0] + s[1] + s[2]) / 3.0
    dx, dy, dz = s[0] - mean, s[1] - mean, s[2] - mean
    second = 0.5 * (dx * dx + dy * dy + dz * dz) + s[3] * s[3] + s[4] * s[4] + s[5] * s[5]
    factor = cohesion / jnp.maximum(jnp.sqrt(second), cohesion)
    pressure = (u_ref[0] + u_ref[1] + u_ref[2]) / 3.0
    out = [pressure + factor * (u_ref[i] - pressure) for i in range(3)]
    out += [factor * u_ref[i] for i in range(3, 6)]
    return out + [u_ref[i] for i in range(6, NQ)]


def place(width, offset, rows):
    r = lax.broadcasted_iota(jnp.int32, (rows, width), 0)
    return (lanes((rows, width)) == r + offset).astype(F32)


def weigh(series, end, begin, q):
    total = None
    for k in range(ORDER):
        term = (end ** (k + 1) - begin ** (k + 1)) / math.factorial(k + 1) * series[k, q]
        total = term if total is None else total + term
    return total


def slot_row(table, one_up, two_up):
    values = table[...].astype(F32).astype(BF16)
    total = None
    for k, (here, there, up) in enumerate(
            ((2, 1, one_up), (1, 2, one_up), (3, 0, two_up), (0, 3, two_up))):
        spread = dot(values, place(LN, 32 * k, 32).astype(BF16))
        row = jnp.where(up, spread[here:here + 1], spread[there:there + 1])
        total = row if total is None else total + row
    return total.astype(jnp.int32)


def first_kernel(*refs):
    ins, outs, scratch = refs[:15], refs[15:36], refs[36:]
    (s_out, w2_out, p2_out, series, piece, t_out, m0, m1, m2, m3, se_out, sf_out, nb_out) = outs[:13]
    fm_out, fp_out, nf_out, or_out, coh_out, fine_out, lift_out, turn_out = outs[13:]
    star, stiff, proj, se, sf, nb, sems = scratch
    places = (series.at[0], star, fm_out, fp_out, coh_out, stiff, proj, lift_out, turn_out, fine_out, nb,
              nf_out, or_out, se, sf)
    copies = [pltpu.make_async_copy(a, b, sems.at[n]) for n, (a, b) in enumerate(zip(ins, places))]
    early = (5, 1, 0, 6, 13, 14)
    rest = [n for n in range(15) if n not in early]
    for n in early:
        copies[n].start()
    for n in rest:
        copies[n].start()
    copies[5].wait()
    minus = [0.5 * (jnp.transpose(stiff[c]) - stiff[c]) for c in range(3)]
    w2_out[...] = two_rows(jnp.concatenate(minus, axis=1), 64)
    copies[1].wait()
    for q in range(NQ):
        for p in range(q + 1):
            s_out[q, p] = 0.5 * (star[q, p] + star[p, q])
            if p != q:
                s_out[p, q] = s_out[q, p]
    copies[0].wait()
    for q in range(NQ):
        piece[q] = series[0, q] * (1.0 / RATE)

    def step(k, weight):
        weight = weight * (1.0 / RATE / (k.astype(F32) + 2.0))
        rows = operator(series.at[k], s_out, w2_out[...])
        for q in range(NQ):
            series[k + 1, q] = rows[q]
            piece[q] += weight * rows[q]
        return weight

    lax.fori_loop(0, ORDER - 1, step, jnp.float32(1.0 / RATE))
    for n in (6, 13, 14):
        copies[n].wait()
    faces = []
    for f in range(4):
        faces += [proj[:, f, :], jnp.zeros((FR - proj.shape[0], NB), F32)]
    p2_out[...] = two_rows(jnp.concatenate(faces, axis=0), FA)
    me = lax.axis_index("dom")
    one_up = lax.rem(me, 2) == 0
    two_up = lax.rem(me, 4) < 2
    se_out[...] = slot_row(se, one_up, two_up)
    sf_out[...] = slot_row(sf, one_up, two_up)
    traces(piece, p2_out[...], t_out)
    send(t_out, se_out, sf_out, (m0, m1, m2, m3))
    for n in rest:
        copies[n].wait()
    two = jnp.where(one_up, 0, 1)
    three = jnp.where(two_up, 2, 3)
    ghost = nb[...] - LN
    block, slot = ghost >> 5, ghost & 31
    place_of = jnp.where(
        block == 2, two, jnp.where(block == 1, 1 - two, jnp.where(block == 3, three, 5 - three)))
    nb_out[...] = jnp.where((ghost >= 0) & (ghost < LN), LN + place_of * 32 + slot, nb[...])


def lift_kernel(lift, rotate, l2_out, lr2_out):
    gap = jnp.zeros((FR - lift.shape[0], NB), F32)
    own, turned = [], [[] for _ in range(3)]
    turns = [jnp.transpose(rotate[k]) for k in range(3)]
    for f in range(4):
        flipped = lift[:, f, :]
        own += [flipped, gap]
        for k in range(3):
            turned[k] += [exact(turns[k], flipped), gap]
    l2_out[...] = two_rows(jnp.transpose(jnp.concatenate(own, axis=0)), 64)
    for k in range(3):
        lr2_out[k] = two_rows(jnp.transpose(jnp.concatenate(turned[k], axis=0)), 64)


def coarse_kernel(series, s_ref, w2, p2, fm_ref, l2, after, u_out, full, t_full):
    del after
    for q in range(NQ):
        full[q] = weigh(series, 1.0, 0.0, q)
    traces(full, p2[...], t_full)
    rows = operator(full, s_ref, w2[...])
    for q in range(NQ):
        u_out[q] = series[0, q] + rows[q] - own_term(fm_ref, t_full, l2[...], q)


def local_kernel(sub, q_ref, pred, t_ref, s_ref, w2, fm_ref, l2, nb_ref, nf_ref, series, u_out,
                 n_out, *next_out):
    rows = operator(pred, s_ref, w2[...])
    for q in range(NQ):
        u_out[q] = q_ref[q] + rows[q] - own_term(fm_ref, t_ref, l2[...], q)
    local_pick(t_ref, nb_ref, nf_ref, n_out)
    if next_out:
        for q in range(NQ):
            next_out[0][q] = weigh(series, (sub + 2) / RATE, (sub + 1) / RATE, q)


def join_kernel(last, *refs):
    (g0, g1, g2, g3, q_ref, u_ref, nl_ref, nacc_ref, fp_ref, lr2, nb_ref, or_ref, coh, fine_ref,
     s_ref, w2, p2, piece, se, sf) = refs[:20]
    table = unpack((g0, g1, g2, g3))
    masks = orient_masks(or_ref)
    fine = fine_ref[...] == 1
    if last:
        uc_ref, out, n_ref, work = refs[20:]
    else:
        q_out, n_out, pred, t_out, m0, m1, m2, m3, n_ref, work, series = refs[20:]

    def face_terms(values):
        for q in range(NQ):
            hi, lo = split(flux_rows(fp_ref, q, n_ref))
            sub = None
            for k in range(3):
                w = lr2[k]
                both = dot(w, hi * masks[k])
                part = both[:NB] + both[64:64 + NB] + dot(w[:64], lo * masks[k])[:NB]
                sub = part if sub is None else sub + part
            work[q] = values(q) - sub

    ghost_pick(table, nb_ref, nl_ref, n_ref)
    if last:
        for q in range(NQ):
            n_ref[q] = jnp.where(fine, n_ref[q], nacc_ref[q] + n_ref[q])
        face_terms(lambda q: jnp.where(fine, u_ref[q], uc_ref[q]))
        after = plastic(work, coh[...])
        for q in range(NQ):
            out[q] = after[q]
        return
    face_terms(lambda q: u_ref[q])
    after = plastic(work, coh[...])
    for q in range(NQ):
        n_out[q] = nacc_ref[q] + n_ref[q] if nacc_ref is not None else n_ref[q]
        x = jnp.where(fine, after[q], q_ref[q])
        q_out[q] = x
        series[q] = x
        pred[q] = x * (1.0 / RATE)

    def step(k, weight):
        weight = weight * (1.0 / RATE / (k.astype(F32) + 2.0))
        rows = operator(series, s_ref, w2[...])
        for q in range(NQ):
            series[q] = rows[q]
            pred[q] += weight * rows[q]
        return weight

    lax.fori_loop(0, ORDER - 1, step, jnp.float32(1.0 / RATE))
    for q in range(NQ):
        pred[q] = jnp.where(fine, pred[q], piece[q])
    traces(pred, p2[...], t_out)
    send(t_out, se, sf, (m0, m1, m2, m3))


BIG = (NQ, NB, LN)
TAB = (NQ, FA, LN)
MSG = (PK, LN)


def call(kernel, name, outs, scratch, args, size=4, space=pltpu.VMEM, limit=24):
    return pl.pallas_call(
        kernel,
        name=name,
        out_shape=[jax.ShapeDtypeStruct(s, d) for s, d in outs],
        in_specs=[pl.BlockSpec(memory_space=space)] * len(args),
        out_specs=[pl.BlockSpec(memory_space=pltpu.VMEM)] * len(outs),
        scratch_shapes=[pltpu.VMEM(*x) if isinstance(x, tuple) else x for x in scratch],
        compiler_params=pltpu.CompilerParams(vmem_limit_bytes=limit << 20),
        cost_estimate=pl.CostEstimate(flops=50_000_000, bytes_accessed=size << 20, transcendentals=0),
    )(*args)


def partners(devices):
    def pairing(step, start, ends):
        pairs = []
        for i in range(devices):
            j = i - start
            t = start + (j ^ step) if j >= 0 else -1
            if t < start or t >= devices:
                t = ends(i)
            pairs.append((i, t))
        return pairs
    return (
        pairing(1, 0, lambda i: i),
        pairing(1, 1, lambda i: devices - 1 - i),
        pairing(2, 0, lambda i: i),
        pairing(2, 2, lambda i: i ^ 1),
    )


def shards(dofs, star, flux_minus, flux_plus, cohesion, stiff, face_proj, lift, rotate, cluster,
           neighbor, neigh_face, orient, send_elem, send_face):
    devices = lax.axis_size("dom")
    pairings = partners(devices)

    def exchange(messages):
        got = [None] * 4
        for k in (2, 3, 1, 0):
            got[k] = lax.ppermute(messages[k], "dom", pairings[k])
        return got

    i32 = jnp.int32
    args = [
        jnp.transpose(dofs, (1, 0, 2)), jnp.transpose(star, (1, 2, 0, 3)),
        jnp.transpose(flux_minus, (1, 2, 0, 3)), jnp.transpose(flux_plus, (1, 2, 0, 3)),
        cohesion.reshape(1, LN), stiff, jnp.transpose(face_proj, (1, 0, 2)),
        jnp.transpose(lift, (2, 0, 1)), rotate, cluster.reshape(1, LN), neighbor, neigh_face,
        orient, send_elem, send_face]
    scratch = [pltpu.VMEM(args[n].shape, args[n].dtype) for n in (1, 5, 6, 13, 14, 10)]
    outs = call(
        first_kernel, "first",
        [((NQ, NQ, 3, LN), F32), ((128, 3 * NB), BF16), ((2 * FA, NB), BF16),
         ((ORDER,) + BIG, F32), (BIG, F32), (TAB, F32)] + [(MSG, F32)] * 4
        + [((1, LN), i32), ((1, LN), i32), ((4, LN), i32), (args[2].shape, F32),
           (args[3].shape, F32), ((4, LN), i32), ((4, LN), i32), ((1, LN), F32), ((1, LN), i32),
           (args[7].shape, F32), (args[8].shape, F32)],
        scratch + [pltpu.SemaphoreType.DMA((15,))],
        [pltpu.with_memory_space_constraint(a, pltpu.HBM) for a in args], space=pltpu.HBM)
    s_mat, w2, p2, series, pred, table = outs[:6]
    got = exchange(outs[6:10])
    se, sf, nb, fm, fp, nf, turn_code, coh, fine, lift, rotate = outs[10:]
    l2, lr2 = call(
        lift_kernel, "lifts", [((128, FA), BF16), ((3, 128, FA), BF16)], [],
        [lift, rotate])
    total = coarse = None
    state = series[0]
    for sub in range(RATE):
        last = sub == RATE - 1
        u, near, *piece = call(
            functools.partial(local_kernel, sub), "local",
            [(BIG, F32), (TAB, F32)] + ([] if last else [(BIG, F32)]), [],
            [state, pred, table, s_mat, w2, fm, l2, nb, nf, series])
        if sub == 1:
            coarse = call(
                coarse_kernel, "coarse_own", [(BIG, F32)], [(BIG, F32), (TAB, F32)],
                [series, s_mat, w2, p2, fm, l2, outs[4]], 8)[0]
        common = [*got, state, u, near, total if total is not None else near, fp, lr2, nb, turn_code,
                  coh, fine, s_mat, w2, p2]
        if last:
            out = call(
                functools.partial(join_kernel, True), "last", [(BIG, F32)],
                [(TAB, F32), (BIG, F32)],
                common + [near, se, sf, coarse])[0]
            return jnp.transpose(out, (1, 0, 2))
        first = total is None

        def kernel(*refs, first=first):
            refs = list(refs)
            if first:
                refs[7] = None
            join_kernel(False, *refs)

        outs = call(
            kernel, "join",
            [(BIG, F32), (TAB, F32), (BIG, F32), (TAB, F32)] + [(MSG, F32)] * 4,
            [(TAB, F32), (BIG, F32), (BIG, F32)],
            common + [piece[0], se, sf])
        state, total, pred, table = outs[:4]
        got = exchange(outs[4:])


def solution(mesh):
    placed = (
        P(None, None, "dom"),
        P(None, None, None, "dom"),
        P(None, None, None, "dom"),
        P(None, None, None, "dom"),
        P("dom"),
        P(),
        P(),
        P(),
        P(),
        P("dom"),
        P(None, "dom"),
        P(None, "dom"),
        P(None, "dom"),
        P(None, "dom"),
        P(None, "dom"),
    )
    return jax.shard_map(
        shards, mesh=mesh, in_specs=placed, out_specs=P(None, None, "dom"), check_vma=False)
```

```python
import functools
import math

import jax
import jax.numpy as jnp
from jax import lax
from jax.experimental import pallas as pl
from jax.experimental.pallas import tpu as pltpu
from jax.sharding import PartitionSpec as P

ORDER = 6
RATE = 4
F32 = jnp.float32
BF16 = jnp.bfloat16
NB = 56
NQ = 9
FR = 24
FA = 4 * FR
LN = 128
PK = 56
PAIRS = 5


def dot(a, b):
    return jnp.dot(a, b, preferred_element_type=F32)


def exact(a, b):
    return jnp.dot(a, b, preferred_element_type=F32, precision=lax.Precision.HIGHEST)


def split(x):
    hi = x.astype(BF16)
    return hi, (x - hi.astype(F32)).astype(BF16)


def two_rows(w):
    hi, lo = split(w)
    return jnp.concatenate([hi.astype(F32), lo.astype(F32)], axis=0).astype(BF16)


def times(w2, rhs, rows):
    hi, lo = split(rhs)
    both = dot(w2, hi)
    return both[:rows] + both[rows:] + dot(w2[:rows], lo)


def side_by_side(w2, halves):
    out = dot(w2, halves)
    return out[:NB, :LN] + out[NB:, :LN] + out[:NB, LN:]


def lift_times(w2, rhs):
    return side_by_side(w2, jnp.concatenate(split(rhs), axis=1))


def star_rows(s_ref, q, which, values):
    total = s_ref[q, 0, which:which + 1, :] * values(0)
    for p in range(1, NQ):
        total = total + s_ref[q, p, which:which + 1, :] * values(p)
    return total


def operator(x_ref, s_ref, w2):
    out = []
    for q in range(NQ):
        stacked = jnp.concatenate(
            [star_rows(s_ref, q, c, lambda p: x_ref[p]) for c in range(3)], axis=0)
        out.append(lift_times(w2, stacked))
    return out


def packed_operator(y_ref, s_ref, w2):
    out = []
    for j in range(PAIRS):
        parts = []
        for c in range(3):
            total = s_ref[j, 0, c:c + 1, :] * y_ref[0]
            for m in range(1, 2 * PAIRS):
                total = total + s_ref[j, m, c:c + 1, :] * y_ref[m]
            parts.append(total)
        out.append(lift_times(w2, jnp.concatenate(parts, axis=0)))
    return out


def both_ways(y_ref, j, rows):
    y_ref[2 * j] = rows
    y_ref[2 * j + 1] = pltpu.roll(rows, LN // 2, 1)


def traces(x_ref, p2, t_ref):
    for q in range(NQ):
        t_ref[q] = times(p2, x_ref[q], FA)


def lanes(shape):
    return lax.broadcasted_iota(jnp.int32, shape, len(shape) - 1)


def pick(rows, index):
    return jnp.take_along_axis(rows, index, axis=1, mode="promise_in_bounds")


def send(t_ref, se_ref, sf_ref, out_refs):
    elem = jnp.broadcast_to(se_ref[...], (FR, LN))
    face = jnp.broadcast_to(sf_ref[...], (FR, LN))
    rows = []
    for q in range(NQ):
        got = pick(t_ref[q, 0:FR], elem)
        for f in range(1, 4):
            got = jnp.where(face == f, pick(t_ref[q, f * FR:(f + 1) * FR], elem), got)
        rows.append(got)
    rows.append(jnp.zeros((4 * PK - NQ * FR, LN), F32))
    table = jnp.concatenate(rows, axis=0)
    group = lanes((PK, LN)) // 32
    for k in range(4):
        message = None
        for g in range(4):
            part = table[g * PK:(g + 1) * PK]
            if g != k:
                part = pltpu.roll(part, ((g - k) * 32) % LN, 1)
            message = part if message is None else jnp.where(group == g, part, message)
        out_refs[k][...] = message


def unpack(in_refs):
    group = lanes((PK, LN)) // 32
    parts = []
    for g in range(4):
        rows = None
        for k in range(4):
            part = in_refs[k][...]
            if g != k:
                part = pltpu.roll(part, ((k - g) * 32) % LN, 1)
            rows = part if rows is None else jnp.where(group == k, part, rows)
        parts.append(rows)
    return jnp.concatenate(parts, axis=0)


def local_pick(t_ref, nb_ref, nf_ref, out_ref):
    for f in range(4):
        where = jnp.broadcast_to(nb_ref[f:f + 1, :], (FR, LN))
        face = jnp.broadcast_to(nf_ref[f:f + 1, :], (FR, LN))
        elem = jnp.minimum(where, LN - 1)
        face = jnp.where(where < LN, face, 4)
        for q in range(NQ):
            got = jnp.zeros((FR, LN), F32)
            for g in range(4):
                got = jnp.where(face == g, pick(t_ref[q, g * FR:(g + 1) * FR], elem), got)
            out_ref[q, f * FR:(f + 1) * FR] = got


def ghost_pick(table, nb_ref, local_ref, out_ref):
    for f in range(4):
        where = jnp.broadcast_to(nb_ref[f:f + 1, :], (FR, LN))
        slot = jnp.clip(where - LN, 0, LN - 1)
        ghost = (where >= LN) & (where < 2 * LN)
        for q in range(NQ):
            got = pick(table[q * FR:(q + 1) * FR], slot)
            out_ref[q, f * FR:(f + 1) * FR] = jnp.where(
                ghost, got, local_ref[q, f * FR:(f + 1) * FR])


def flux_rows(f_ref, q, t_ref):
    return jnp.concatenate(
        [star_rows(f_ref, q, f, lambda p: t_ref[p, f * FR:(f + 1) * FR]) for f in range(4)],
        axis=0)


def own_term(f_ref, t_ref, l2, q):
    return lift_times(l2, flux_rows(f_ref, q, t_ref))


def orient_masks(or_ref):
    codes = jnp.concatenate(
        [jnp.broadcast_to(or_ref[f:f + 1, :], (FR, LN)) for f in range(4)], axis=0)
    masks = [(codes == k).astype(F32).astype(BF16) for k in range(3)]
    return [jnp.concatenate([m, m], axis=1) for m in masks]


def plastic(u_ref, cohesion):
    s = [u_ref[q, 0:1, :] for q in range(6)]
    mean = (s[0] + s[1] + s[2]) / 3.0
    dx, dy, dz = s[0] - mean, s[1] - mean, s[2] - mean
    second = 0.5 * (dx * dx + dy * dy + dz * dz) + s[3] * s[3] + s[4] * s[4] + s[5] * s[5]
    factor = cohesion / jnp.maximum(jnp.sqrt(second), cohesion)
    pressure = (u_ref[0] + u_ref[1] + u_ref[2]) / 3.0
    out = [pressure + factor * (u_ref[i] - pressure) for i in range(3)]
    out += [factor * u_ref[i] for i in range(3, 6)]
    return out + [u_ref[i] for i in range(6, NQ)]


def place(width, offset, rows):
    r = lax.broadcasted_iota(jnp.int32, (rows, width), 0)
    return (lanes((rows, width)) == r + offset).astype(F32)


def weigh(series, end, begin, q):
    total = None
    for k in range(ORDER):
        term = (end ** (k + 1) - begin ** (k + 1)) / math.factorial(k + 1) * series[k, q]
        total = term if total is None else total + term
    return total


def slot_row(table, one_up, two_up):
    values = table[...].astype(F32).astype(BF16)
    total = None
    for k, (here, there, up) in enumerate(
            ((2, 1, one_up), (1, 2, one_up), (3, 0, two_up), (0, 3, two_up))):
        spread = dot(values, place(LN, 32 * k, 32).astype(BF16))
        row = jnp.where(up, spread[here:here + 1], spread[there:there + 1])
        total = row if total is None else total + row
    return total.astype(jnp.int32)


def first_kernel(*refs):
    ins, outs, scratch = refs[:15], refs[15:36], refs[36:]
    (s_out, w2_out, p2_out, series, piece, t_out, m0, m1, m2, m3, se_out, sf_out, nb_out) = outs[:13]
    fm_out, fp_out, nf_out, or_out, coh_out, fine_out, lift_out, turn_out = outs[13:]
    star, stiff, proj, se, sf, nb, sems = scratch
    places = (series.at[0], star, fm_out, fp_out, coh_out, stiff, proj, lift_out, turn_out, fine_out, nb,
              nf_out, or_out, se, sf)
    copies = [pltpu.make_async_copy(a, b, sems.at[n]) for n, (a, b) in enumerate(zip(ins, places))]
    early = (5, 1, 0, 6, 13, 14)
    rest = [n for n in range(15) if n not in early]
    for n in early:
        copies[n].start()
    for n in rest:
        copies[n].start()
    copies[5].wait()
    minus = [0.5 * (jnp.transpose(stiff[c]) - stiff[c]) for c in range(3)]
    w2_out[...] = two_rows(jnp.concatenate(minus, axis=1))
    copies[1].wait()
    for q in range(NQ):
        for p in range(q + 1):
            s_out[q, p] = 0.5 * (star[q, p] + star[p, q])
            if p != q:
                s_out[p, q] = s_out[q, p]
    copies[0].wait()
    for q in range(NQ):
        piece[q] = series[0, q] * (1.0 / RATE)

    for k in range(ORDER - 1):
        weight = (1.0 / RATE) ** (k + 2) / math.factorial(k + 2)
        rows = operator(series.at[k], s_out, w2_out[...])
        for q in range(NQ):
            series[k + 1, q] = rows[q]
            piece[q] += weight * rows[q]
    for n in (6, 13, 14):
        copies[n].wait()
    faces = []
    for f in range(4):
        faces += [proj[:, f, :], jnp.zeros((FR - proj.shape[0], NB), F32)]
    p2_out[...] = two_rows(jnp.concatenate(faces, axis=0))
    me = lax.axis_index("dom")
    one_up = lax.rem(me, 2) == 0
    two_up = lax.rem(me, 4) < 2
    se_out[...] = slot_row(se, one_up, two_up)
    sf_out[...] = slot_row(sf, one_up, two_up)
    traces(piece, p2_out[...], t_out)
    send(t_out, se_out, sf_out, (m0, m1, m2, m3))
    for n in rest:
        copies[n].wait()
    two = jnp.where(one_up, 0, 1)
    three = jnp.where(two_up, 2, 3)
    ghost = nb[...] - LN
    block, slot = ghost >> 5, ghost & 31
    place_of = jnp.where(
        block == 2, two, jnp.where(block == 1, 1 - two, jnp.where(block == 3, three, 5 - three)))
    nb_out[...] = jnp.where((ghost >= 0) & (ghost < LN), LN + place_of * 32 + slot, nb[...])


def lift_kernel(lift, rotate, s_ref, fine_ref, l2_out, lr2_out, order_out, spot_out, pack_out, rows):
    is_fine = jnp.broadcast_to(fine_ref[...], (LN, LN))
    down = lax.broadcasted_iota(jnp.int32, (LN, LN), 0)
    across = lanes((LN, LN))
    ahead = (down < across).astype(F32).astype(BF16)
    spot = dot(is_fine.astype(F32).astype(BF16), ahead)
    own_spot = jnp.transpose(spot).astype(jnp.int32)
    own_fine = jnp.transpose(is_fine.astype(F32)) > 0.5
    chosen = own_fine & (own_spot == across % (LN // 2))
    order = dot(across.astype(F32).astype(BF16), chosen.astype(F32).astype(BF16)).astype(jnp.int32)
    order_out[...] = order[0:8]
    low = jnp.minimum(spot.astype(jnp.int32), LN // 2 - 1)
    spot_out[0] = low[0:8]
    spot_out[1] = low[0:8] + LN // 2
    order = order[0:8]
    for q in range(NQ):
        for p in range(q + 1):
            got = pick(jnp.concatenate([s_ref[q, p], jnp.zeros((5, LN), F32)], axis=0), order)
            rows[q, p] = got
            rows[p, q] = got
    left = lanes((3, LN)) < LN // 2

    def entry(q, p):
        return rows[q, p, 0:3] if q < NQ and p < NQ else jnp.zeros((3, LN), F32)

    for j in range(PAIRS):
        for i in range(PAIRS):
            a, b = 2 * j, 2 * i
            pack_out[j, b] = jnp.where(left, entry(a, b), entry(a + 1, b + 1))
            pack_out[j, b + 1] = jnp.where(left, entry(a, b + 1), entry(a + 1, b))
    gap = jnp.zeros((FR - lift.shape[0], NB), F32)
    own, turned = [], [[] for _ in range(3)]
    turns = [jnp.transpose(rotate[k]) for k in range(3)]
    for f in range(4):
        flipped = lift[:, f, :]
        own += [flipped, gap]
        for k in range(3):
            turned[k] += [exact(turns[k], flipped), gap]
    l2_out[...] = two_rows(jnp.transpose(jnp.concatenate(own, axis=0)))
    lr2_out[...] = two_rows(jnp.transpose(jnp.concatenate(turned[0] + turned[1] + turned[2], axis=0)))


def coarse_kernel(series, s_ref, w2, p2, fm_ref, l2, after, u_out, full, t_full):
    del after
    for q in range(NQ):
        full[q] = weigh(series, 1.0, 0.0, q)
    traces(full, p2[...], t_full)
    rows = operator(full, s_ref, w2[...])
    for q in range(NQ):
        u_out[q] = series[0, q] + rows[q] - own_term(fm_ref, t_full, l2[...], q)


def local_kernel(sub, q_ref, pred, t_ref, s_ref, w2, fm_ref, l2, nb_ref, nf_ref, series, u_out,
                 n_out, *next_out):
    rows = operator(pred, s_ref, w2[...])
    for q in range(NQ):
        u_out[q] = q_ref[q] + rows[q] - own_term(fm_ref, t_ref, l2[...], q)
    local_pick(t_ref, nb_ref, nf_ref, n_out)
    if next_out:
        for q in range(NQ):
            next_out[0][q] = weigh(series, (sub + 2) / RATE, (sub + 1) / RATE, q)


def join_kernel(last, *refs):
    (g2, g3, g1, g0, q_ref, u_ref, nl_ref, nacc_ref, fp_ref, lr2, nb_ref, or_ref, coh, fine_ref,
     pack_ref, w2, p2, piece, se, sf, order_ref, spot_ref) = refs[:22]
    table = unpack((g0, g1, g2, g3))
    masks = orient_masks(or_ref)
    fine = fine_ref[...] == 1
    if last:
        uc_ref, out, n_ref, work = refs[22:]
    else:
        q_out, n_out, pred, t_out, m0, m1, m2, m3, n_ref, work, series, sums = refs[22:]

    def face_terms(values):
        for q in range(NQ):
            halves = jnp.concatenate(split(flux_rows(fp_ref, q, n_ref)), axis=1)
            sub = side_by_side(lr2[...], jnp.concatenate([halves * m for m in masks], axis=0))
            work[q] = values(q) - sub

    ghost_pick(table, nb_ref, nl_ref, n_ref)
    if last:
        for q in range(NQ):
            n_ref[q] = jnp.where(fine, n_ref[q], nacc_ref[q] + n_ref[q])
        face_terms(lambda q: jnp.where(fine, u_ref[q], uc_ref[q]))
        after = plastic(work, coh[...])
        for q in range(NQ):
            out[q] = after[q]
        return
    face_terms(lambda q: u_ref[q])
    after = plastic(work, coh[...])
    for q in range(NQ):
        n_out[q] = nacc_ref[q] + n_ref[q] if nacc_ref is not None else n_ref[q]
        x = jnp.where(fine, after[q], q_ref[q])
        q_out[q] = x
    order = jnp.broadcast_to(order_ref[0:1, :], (NB, LN))
    left = lanes((NB, LN)) < LN // 2
    for j in range(PAIRS):
        rows = pick(q_out[2 * j], order)
        other = pick(q_out[2 * j + 1], order) if 2 * j + 1 < NQ else jnp.zeros((NB, LN), F32)
        rows = jnp.where(left, rows, other)
        both_ways(series.at[0], j, rows)
        sums[j] = rows * (1.0 / RATE)

    for k in range(ORDER - 1):
        weight = (1.0 / RATE) ** (k + 2) / math.factorial(k + 2)
        rows = packed_operator(series.at[k % 2], pack_ref, w2[...])
        for j in range(PAIRS):
            if k < ORDER - 2:
                both_ways(series.at[(k + 1) % 2], j, rows[j])
            sums[j] += weight * rows[j]
    for q in range(NQ):
        spot = jnp.broadcast_to(spot_ref[q % 2, 0:1, :], (NB, LN))
        pred[q] = jnp.where(fine, pick(sums[q // 2], spot), piece[q])
    traces(pred, p2[...], t_out)
    send(t_out, se, sf, (m0, m1, m2, m3))


BIG = (NQ, NB, LN)
TAB = (NQ, FA, LN)
MSG = (PK, LN)


def call(kernel, name, outs, scratch, args, size=4, space=pltpu.VMEM, limit=24):
    return pl.pallas_call(
        kernel,
        name=name,
        out_shape=[jax.ShapeDtypeStruct(s, d) for s, d in outs],
        in_specs=[pl.BlockSpec(memory_space=space)] * len(args),
        out_specs=[pl.BlockSpec(memory_space=pltpu.VMEM)] * len(outs),
        scratch_shapes=[pltpu.VMEM(*x) if isinstance(x, tuple) else x for x in scratch],
        compiler_params=pltpu.CompilerParams(vmem_limit_bytes=limit << 20),
        cost_estimate=pl.CostEstimate(flops=50_000_000, bytes_accessed=size << 20, transcendentals=0),
    )(*args)


def partners(devices):
    def pairing(step, start, ends):
        pairs = []
        for i in range(devices):
            j = i - start
            t = start + (j ^ step) if j >= 0 else -1
            if t < start or t >= devices:
                t = ends(i)
            pairs.append((i, t))
        return pairs
    return (
        pairing(1, 0, lambda i: i),
        pairing(1, 1, lambda i: devices - 1 - i),
        pairing(2, 0, lambda i: i),
        pairing(2, 2, lambda i: i ^ 1),
    )


def shards(dofs, star, flux_minus, flux_plus, cohesion, stiff, face_proj, lift, rotate, cluster,
           neighbor, neigh_face, orient, send_elem, send_face):
    devices = lax.axis_size("dom")
    pairings = partners(devices)

    def exchange(messages):
        got = [None] * 4
        for k in (2, 3, 1, 0):
            got[k] = lax.ppermute(messages[k], "dom", pairings[k])
        return got

    i32 = jnp.int32
    args = [
        jnp.transpose(dofs, (1, 0, 2)), jnp.transpose(star, (1, 2, 0, 3)),
        jnp.transpose(flux_minus, (1, 2, 0, 3)), jnp.transpose(flux_plus, (1, 2, 0, 3)),
        cohesion.reshape(1, LN), stiff, jnp.transpose(face_proj, (1, 0, 2)),
        jnp.transpose(lift, (2, 0, 1)), rotate, cluster.reshape(1, LN), neighbor, neigh_face,
        orient, send_elem, send_face]
    scratch = [pltpu.VMEM(args[n].shape, args[n].dtype) for n in (1, 5, 6, 13, 14, 10)]
    outs = call(
        first_kernel, "first",
        [((NQ, NQ, 3, LN), F32), ((2 * NB, 3 * NB), BF16), ((2 * FA, NB), BF16),
         ((ORDER,) + BIG, F32), (BIG, F32), (TAB, F32)] + [(MSG, F32)] * 4
        + [((1, LN), i32), ((1, LN), i32), ((4, LN), i32), (args[2].shape, F32),
           (args[3].shape, F32), ((4, LN), i32), ((4, LN), i32), ((1, LN), F32), ((1, LN), i32),
           (args[7].shape, F32), (args[8].shape, F32)],
        scratch + [pltpu.SemaphoreType.DMA((15,))],
        [pltpu.with_memory_space_constraint(a, pltpu.HBM) for a in args], space=pltpu.HBM)
    s_mat, w2, p2, series, pred, table = outs[:6]
    got = exchange(outs[6:10])
    se, sf, nb, fm, fp, nf, turn_code, coh, fine, lift, rotate = outs[10:]
    l2, lr2, order, spot, pack = call(
        lift_kernel, "lifts",
        [((2 * NB, FA), BF16), ((2 * NB, 3 * FA), BF16), ((8, LN), i32), ((2, 8, LN), i32),
         ((PAIRS, 2 * PAIRS, 3, LN), F32)],
        [((NQ, NQ, 8, LN), F32)],
        [lift, rotate, s_mat, fine])
    total = coarse = None
    state = series[0]
    for sub in range(RATE):
        last = sub == RATE - 1
        u, near, *piece = call(
            functools.partial(local_kernel, sub), "local",
            [(BIG, F32), (TAB, F32)] + ([] if last else [(BIG, F32)]), [],
            [state, pred, table, s_mat, w2, fm, l2, nb, nf, series])
        if sub == 1:
            coarse = call(
                coarse_kernel, "coarse_own", [(BIG, F32)], [(BIG, F32), (TAB, F32)],
                [series, s_mat, w2, p2, fm, l2, outs[4]], 8)[0]
        common = [got[2], got[3], got[1], got[0], state, u, near, total if total is not None else near, fp, lr2, nb, turn_code,
                  coh, fine, pack, w2, p2]
        if last:
            out = call(
                functools.partial(join_kernel, True), "last", [(BIG, F32)],
                [(TAB, F32), (BIG, F32)],
                common + [near, se, sf, order, spot, coarse])[0]
            return jnp.transpose(out, (1, 0, 2))
        first = total is None

        def kernel(*refs, first=first):
            refs = list(refs)
            if first:
                refs[7] = None
            join_kernel(False, *refs)

        outs = call(
            kernel, "join",
            [(BIG, F32), (TAB, F32), (BIG, F32), (TAB, F32)] + [(MSG, F32)] * 4,
            [(TAB, F32), (BIG, F32), ((2, 2 * PAIRS, NB, LN), F32), ((PAIRS, NB, LN), F32)],
            common + [piece[0], se, sf, order, spot])
        state, total, pred, table = outs[:4]
        got = exchange(outs[4:])


def solution(mesh):
    placed = (
        P(None, None, "dom"),
        P(None, None, None, "dom"),
        P(None, None, None, "dom"),
        P(None, None, None, "dom"),
        P("dom"),
        P(),
        P(),
        P(),
        P(),
        P("dom"),
        P(None, "dom"),
        P(None, "dom"),
        P(None, "dom"),
        P(None, "dom"),
        P(None, "dom"),
    )
    return jax.shard_map(
        shards, mesh=mesh, in_specs=placed, out_specs=P(None, None, "dom"), check_vma=False)
```

```python
import functools
import math

import jax
import jax.numpy as jnp
from jax import lax
from jax.experimental import pallas as pl
from jax.experimental.pallas import tpu as pltpu
from jax.sharding import PartitionSpec as P

ORDER = 6
RATE = 4
F32 = jnp.float32
BF16 = jnp.bfloat16
NB = 56
NQ = 9
FR = 24
FA = 4 * FR
LN = 128
PK = 56
PAIRS = 5


def dot(a, b):
    return jnp.dot(a, b, preferred_element_type=F32)


def exact(a, b):
    return jnp.dot(a, b, preferred_element_type=F32, precision=lax.Precision.HIGHEST)


def split(x):
    hi = x.astype(BF16)
    return hi, (x - hi.astype(F32)).astype(BF16)


def two_rows(w):
    hi, lo = split(w)
    return jnp.concatenate([hi.astype(F32), lo.astype(F32)], axis=0).astype(BF16)


def times(w2, rhs, rows):
    hi, lo = split(rhs)
    both = dot(w2, hi)
    return both[:rows] + both[rows:] + dot(w2[:rows], lo)


def side_by_side(w2, halves):
    out = dot(w2, halves)
    return out[:NB, :LN] + out[NB:, :LN] + out[:NB, LN:]


def lift_times(w2, rhs):
    return side_by_side(w2, jnp.concatenate(split(rhs), axis=1))


def star_rows(s_ref, q, which, values):
    total = s_ref[q, 0, which:which + 1, :] * values(0)
    for p in range(1, NQ):
        total = total + s_ref[q, p, which:which + 1, :] * values(p)
    return total


def operator(x_ref, s_ref, w2):
    out = []
    for q in range(NQ):
        stacked = jnp.concatenate(
            [star_rows(s_ref, q, c, lambda p: x_ref[p]) for c in range(3)], axis=0)
        out.append(lift_times(w2, stacked))
    return out


def packed_operator(y_ref, s_ref, w2):
    out = []
    for j in range(PAIRS):
        parts = []
        for c in range(3):
            total = s_ref[j, 0, c:c + 1, :] * y_ref[0]
            for m in range(1, 2 * PAIRS):
                total = total + s_ref[j, m, c:c + 1, :] * y_ref[m]
            parts.append(total)
        out.append(lift_times(w2, jnp.concatenate(parts, axis=0)))
    return out


def both_ways(y_ref, j, rows):
    y_ref[2 * j] = rows
    y_ref[2 * j + 1] = pltpu.roll(rows, LN // 2, 1)


def traces(x_ref, p2, t_ref):
    for q in range(NQ):
        t_ref[q] = times(p2, x_ref[q], FA)


def lanes(shape):
    return lax.broadcasted_iota(jnp.int32, shape, len(shape) - 1)


def pick(rows, index):
    return jnp.take_along_axis(rows, index, axis=1, mode="promise_in_bounds")


def chosen_face(face, rows):
    got = rows(0)
    for f in range(1, 4):
        got = jnp.where(face == f, rows(f), got)
    return got


def pack(rows, out_refs):
    table = jnp.concatenate(rows + [jnp.zeros((4 * PK - NQ * FR, LN), F32)], axis=0)
    group = lanes((PK, LN)) // 32
    for k in range(4):
        message = None
        for g in range(4):
            part = table[g * PK:(g + 1) * PK]
            if g != k:
                part = pltpu.roll(part, ((g - k) * 32) % LN, 1)
            message = part if message is None else jnp.where(group == g, part, message)
        out_refs[k][...] = message


def send(t_ref, se_ref, sf_ref, out_refs):
    elem = jnp.broadcast_to(se_ref[...], (FR, LN))
    face = jnp.broadcast_to(sf_ref[...], (FR, LN))
    pack([chosen_face(face, lambda f: pick(t_ref[q, f * FR:(f + 1) * FR], elem))
          for q in range(NQ)], out_refs)


def send_packed(t_ref, coarse_ref, spot_ref, slot_fine, sf_ref, out_refs):
    face = jnp.broadcast_to(sf_ref[...], (FR, LN))
    is_fine = jnp.broadcast_to(slot_fine[0:1, :], (FR, LN)) == 1
    rows = []
    for q in range(NQ):
        spot = jnp.broadcast_to(spot_ref[q % 2, 0:1, :], (FR, LN))
        got = chosen_face(face, lambda f: pick(t_ref[q // 2, f * FR:(f + 1) * FR], spot))
        rows.append(jnp.where(is_fine, got, coarse_ref[q]))
    pack(rows, out_refs)


def unpack(in_refs):
    group = lanes((PK, LN)) // 32
    parts = []
    for g in range(4):
        rows = None
        for k in range(4):
            part = in_refs[k][...]
            if g != k:
                part = pltpu.roll(part, ((k - g) * 32) % LN, 1)
            rows = part if rows is None else jnp.where(group == k, part, rows)
        parts.append(rows)
    return jnp.concatenate(parts, axis=0)


def local_pick(t_ref, nb_ref, nf_ref, out_ref):
    for f in range(4):
        where = jnp.broadcast_to(nb_ref[f:f + 1, :], (FR, LN))
        face = jnp.broadcast_to(nf_ref[f:f + 1, :], (FR, LN))
        elem = jnp.minimum(where, LN - 1)
        face = jnp.where(where < LN, face, 4)
        for q in range(NQ):
            got = jnp.zeros((FR, LN), F32)
            for g in range(4):
                got = jnp.where(face == g, pick(t_ref[q, g * FR:(g + 1) * FR], elem), got)
            out_ref[q, f * FR:(f + 1) * FR] = got


def ghost_rows(values, nb_ref):
    out = []
    for f in range(4):
        where = jnp.broadcast_to(nb_ref[f:f + 1, :], (FR, LN))
        slot = jnp.clip(where - LN, 0, LN - 1)
        ghost = (where >= LN) & (where < 2 * LN)
        out.append(jnp.where(ghost, pick(values, slot), 0.0))
    return jnp.concatenate(out, axis=0)


def turned_lift(lr2, masks, rows):
    halves = jnp.concatenate(split(rows), axis=1)
    return side_by_side(lr2, jnp.concatenate([halves * m for m in masks], axis=0))


def flux_rows(f_ref, q, t_ref):
    return jnp.concatenate(
        [star_rows(f_ref, q, f, lambda p: t_ref[p, f * FR:(f + 1) * FR]) for f in range(4)],
        axis=0)


def own_term(f_ref, t_ref, l2, q):
    return lift_times(l2, flux_rows(f_ref, q, t_ref))


def orient_masks(or_ref):
    codes = jnp.concatenate(
        [jnp.broadcast_to(or_ref[f:f + 1, :], (FR, LN)) for f in range(4)], axis=0)
    masks = [(codes == k).astype(F32).astype(BF16) for k in range(3)]
    return [jnp.concatenate([m, m], axis=1) for m in masks]


def plastic(u_ref, cohesion):
    s = [u_ref[q, 0:1, :] for q in range(6)]
    mean = (s[0] + s[1] + s[2]) / 3.0
    dx, dy, dz = s[0] - mean, s[1] - mean, s[2] - mean
    second = 0.5 * (dx * dx + dy * dy + dz * dz) + s[3] * s[3] + s[4] * s[4] + s[5] * s[5]
    factor = cohesion / jnp.maximum(jnp.sqrt(second), cohesion)
    pressure = (u_ref[0] + u_ref[1] + u_ref[2]) / 3.0
    out = [pressure + factor * (u_ref[i] - pressure) for i in range(3)]
    out += [factor * u_ref[i] for i in range(3, 6)]
    return out + [u_ref[i] for i in range(6, NQ)]


def place(width, offset, rows):
    r = lax.broadcasted_iota(jnp.int32, (rows, width), 0)
    return (lanes((rows, width)) == r + offset).astype(F32)


def weigh(series, end, begin, q):
    total = None
    for k in range(ORDER):
        term = (end ** (k + 1) - begin ** (k + 1)) / math.factorial(k + 1) * series[k, q]
        total = term if total is None else total + term
    return total


def slot_row(table, one_up, two_up):
    values = table[...].astype(F32).astype(BF16)
    total = None
    for k, (here, there, up) in enumerate(
            ((2, 1, one_up), (1, 2, one_up), (3, 0, two_up), (0, 3, two_up))):
        spread = dot(values, place(LN, 32 * k, 32).astype(BF16))
        row = jnp.where(up, spread[here:here + 1], spread[there:there + 1])
        total = row if total is None else total + row
    return total.astype(jnp.int32)


def first_kernel(*refs):
    ins, outs, scratch = refs[:15], refs[15:36], refs[36:]
    (s_out, w2_out, p2_out, series, piece, t_out, m0, m1, m2, m3, se_out, sf_out, nb_out) = outs[:13]
    fm_out, fp_out, nf_out, or_out, coh_out, fine_out, lift_out, turn_out = outs[13:]
    star, stiff, proj, se, sf, nb, sems = scratch
    places = (series.at[0], star, fm_out, fp_out, coh_out, stiff, proj, lift_out, turn_out, fine_out, nb,
              nf_out, or_out, se, sf)
    copies = [pltpu.make_async_copy(a, b, sems.at[n]) for n, (a, b) in enumerate(zip(ins, places))]
    early = (5, 1, 0, 6, 13, 14)
    rest = [n for n in range(15) if n not in early]
    for n in early:
        copies[n].start()
    for n in rest:
        copies[n].start()
    copies[5].wait()
    minus = [0.5 * (jnp.transpose(stiff[c]) - stiff[c]) for c in range(3)]
    w2_out[...] = two_rows(jnp.concatenate(minus, axis=1))
    copies[1].wait()
    for q in range(NQ):
        for p in range(q + 1):
            s_out[q, p] = 0.5 * (star[q, p] + star[p, q])
            if p != q:
                s_out[p, q] = s_out[q, p]
    copies[0].wait()
    for q in range(NQ):
        piece[q] = series[0, q] * (1.0 / RATE)

    for k in range(ORDER - 1):
        weight = (1.0 / RATE) ** (k + 2) / math.factorial(k + 2)
        rows = operator(series.at[k], s_out, w2_out[...])
        for q in range(NQ):
            series[k + 1, q] = rows[q]
            piece[q] += weight * rows[q]
    for n in (6, 13, 14):
        copies[n].wait()
    faces = []
    for f in range(4):
        faces += [proj[:, f, :], jnp.zeros((FR - proj.shape[0], NB), F32)]
    p2_out[...] = two_rows(jnp.concatenate(faces, axis=0))
    me = lax.axis_index("dom")
    one_up = lax.rem(me, 2) == 0
    two_up = lax.rem(me, 4) < 2
    se_out[...] = slot_row(se, one_up, two_up)
    sf_out[...] = slot_row(sf, one_up, two_up)
    traces(piece, p2_out[...], t_out)
    send(t_out, se_out, sf_out, (m0, m1, m2, m3))
    for n in rest:
        copies[n].wait()
    two = jnp.where(one_up, 0, 1)
    three = jnp.where(two_up, 2, 3)
    ghost = nb[...] - LN
    block, slot = ghost >> 5, ghost & 31
    place_of = jnp.where(
        block == 2, two, jnp.where(block == 1, 1 - two, jnp.where(block == 3, three, 5 - three)))
    nb_out[...] = jnp.where((ghost >= 0) & (ghost < LN), LN + place_of * 32 + slot, nb[...])


def lift_kernel(lift, rotate, s_ref, fine_ref, se_ref, nb_ref, fp_ref, l2_out, lr2_out, order_out,
                spot_out, pack_out, slot_spot, slot_fine, slot_flux, rows):
    is_fine = jnp.broadcast_to(fine_ref[...], (LN, LN))
    down = lax.broadcasted_iota(jnp.int32, (LN, LN), 0)
    across = lanes((LN, LN))
    ahead = (down < across).astype(F32).astype(BF16)
    spot = dot(is_fine.astype(F32).astype(BF16), ahead)
    own_spot = jnp.transpose(spot).astype(jnp.int32)
    own_fine = jnp.transpose(is_fine.astype(F32)) > 0.5
    chosen = own_fine & (own_spot == across % (LN // 2))
    order = dot(across.astype(F32).astype(BF16), chosen.astype(F32).astype(BF16)).astype(jnp.int32)
    order_out[...] = order[0:8]
    low = jnp.minimum(spot.astype(jnp.int32), LN // 2 - 1)
    spot_out[0] = low[0:8]
    spot_out[1] = low[0:8] + LN // 2
    order = order[0:8]
    elem = jnp.broadcast_to(se_ref[...], (8, LN))
    slot_spot[0] = pick(low[0:8], elem)
    slot_spot[1] = slot_spot[0] + LN // 2
    slot_fine[...] = pick(jnp.broadcast_to(fine_ref[...], (8, LN)), elem)
    target = face = jnp.zeros((LN, LN), F32)
    for f in range(4):
        named = jnp.transpose(jnp.broadcast_to(nb_ref[f:f + 1, :], (LN, LN)).astype(F32))
        hit = (named == (across + LN).astype(F32)).astype(F32).astype(BF16)
        target = target + dot(across.astype(F32).astype(BF16), hit)
        face = face + f * dot(jnp.ones((LN, LN), BF16), hit)
    target = target[0:8].astype(jnp.int32)
    face = face[0:1].astype(jnp.int32)
    for q in range(NQ):
        for p in range(NQ):
            got = pick(jnp.concatenate([fp_ref[q, p], jnp.zeros((4, LN), F32)], axis=0), target)
            slot_flux[q, p:p + 1, :] = chosen_face(face, lambda f: got[f:f + 1])
    for q in range(NQ):
        for p in range(q + 1):
            got = pick(jnp.concatenate([s_ref[q, p], jnp.zeros((5, LN), F32)], axis=0), order)
            rows[q, p] = got
            rows[p, q] = got
    left = lanes((3, LN)) < LN // 2

    def entry(q, p):
        return rows[q, p, 0:3] if q < NQ and p < NQ else jnp.zeros((3, LN), F32)

    for j in range(PAIRS):
        for i in range(PAIRS):
            a, b = 2 * j, 2 * i
            pack_out[j, b] = jnp.where(left, entry(a, b), entry(a + 1, b + 1))
            pack_out[j, b + 1] = jnp.where(left, entry(a, b + 1), entry(a + 1, b))
    gap = jnp.zeros((FR - lift.shape[0], NB), F32)
    own, turned = [], [[] for _ in range(3)]
    turns = [jnp.transpose(rotate[k]) for k in range(3)]
    for f in range(4):
        flipped = lift[:, f, :]
        own += [flipped, gap]
        for k in range(3):
            turned[k] += [exact(turns[k], flipped), gap]
    l2_out[...] = two_rows(jnp.transpose(jnp.concatenate(own, axis=0)))
    lr2_out[...] = two_rows(jnp.transpose(jnp.concatenate(turned[0] + turned[1] + turned[2], axis=0)))


def coarse_kernel(series, s_ref, w2, p2, fm_ref, l2, after, u_out, full, t_full):
    del after
    for q in range(NQ):
        full[q] = weigh(series, 1.0, 0.0, q)
    traces(full, p2[...], t_full)
    rows = operator(full, s_ref, w2[...])
    for q in range(NQ):
        u_out[q] = series[0, q] + rows[q] - own_term(fm_ref, t_full, l2[...], q)


def local_kernel(sub, *refs):
    (q_ref, s_ref, w2, p2, fm_ref, l2, fp_ref, lr2, nb_ref, nf_ref, or_ref, series, se, sf, fine_ref,
     spot_ref) = refs[:16]
    if sub == 0:
        pred, t_ref = refs[16:18]
        rest = refs[18:]
    else:
        sums, piece = refs[16:18]
        pred, t_ref = refs[-2:]
        rest = refs[18:-2]
        fine = fine_ref[...] == 1
        for q in range(NQ):
            spot = jnp.broadcast_to(spot_ref[q % 2, 0:1, :], (NB, LN))
            pred[q] = jnp.where(fine, pick(sums[q // 2], spot), piece[q])
        traces(pred, p2[...], t_ref)
    u_out, near_out, *coming, n_ref = rest
    rows = operator(pred, s_ref, w2[...])
    for q in range(NQ):
        u_out[q] = q_ref[q] + rows[q] - own_term(fm_ref, t_ref, l2[...], q)
    local_pick(t_ref, nb_ref, nf_ref, n_ref)
    masks = orient_masks(or_ref)
    for q in range(NQ):
        near_out[q] = turned_lift(lr2[...], masks, flux_rows(fp_ref, q, n_ref))
    if coming:
        piece_out, slots_out = coming
        elem = jnp.broadcast_to(se[...], (NB, LN))
        face = jnp.broadcast_to(sf[...], (FR, LN))
        for q in range(NQ):
            values = weigh(series, (sub + 2) / RATE, (sub + 1) / RATE, q)
            piece_out[q] = values
            table = times(p2[...], pick(values, elem), FA)
            slots_out[q] = chosen_face(face, lambda f: table[f * FR:(f + 1) * FR])


def ghost_terms(refs):
    (g2, g3, g1, g0, flux, lr2, nb_ref, or_ref) = refs
    table = unpack((g0, g1, g2, g3))
    masks = orient_masks(or_ref)
    for q in range(NQ):
        total = flux[q, 0:1, :] * table[:FR]
        for p in range(1, NQ):
            total = total + flux[q, p:p + 1, :] * table[p * FR:(p + 1) * FR]
        yield q, turned_lift(lr2[...], masks, ghost_rows(total, nb_ref))


def last_kernel(*refs):
    u_ref, near, acc, uc_ref, coh, fine_ref, out, work = refs[8:]
    fine = fine_ref[...] == 1
    for q, term in ghost_terms(refs[:8]):
        work[q] = jnp.where(fine, u_ref[q], uc_ref[q] - acc[q]) - near[q] - term
    after = plastic(work, coh[...])
    for q in range(NQ):
        out[q] = after[q]


def join_kernel(first, *refs):
    (u_ref, near, acc, coh, fine_ref, q_ref, pack_ref, w2, p2, slots, sf, order_ref, spot_ref,
     slot_fine, q_out, acc_out, sums, m0, m1, m2, m3, work, series, t_ref) = refs[8:]
    fine = fine_ref[...] == 1
    for q, term in ghost_terms(refs[:8]):
        term = near[q] + term
        work[q] = u_ref[q] - term
        acc_out[q] = term if first else acc[q] + term
    after = plastic(work, coh[...])
    for q in range(NQ):
        q_out[q] = jnp.where(fine, after[q], q_ref[q])
    order = jnp.broadcast_to(order_ref[0:1, :], (NB, LN))
    left = lanes((NB, LN)) < LN // 2
    for j in range(PAIRS):
        rows = pick(q_out[2 * j], order)
        other = pick(q_out[2 * j + 1], order) if 2 * j + 1 < NQ else jnp.zeros((NB, LN), F32)
        rows = jnp.where(left, rows, other)
        both_ways(series.at[0], j, rows)
        sums[j] = rows * (1.0 / RATE)
    for k in range(ORDER - 1):
        weight = (1.0 / RATE) ** (k + 2) / math.factorial(k + 2)
        rows = packed_operator(series.at[k % 2], pack_ref, w2[...])
        for j in range(PAIRS):
            if k < ORDER - 2:
                both_ways(series.at[(k + 1) % 2], j, rows[j])
            sums[j] += weight * rows[j]
    for j in range(PAIRS):
        t_ref[j] = times(p2[...], sums[j], FA)
    send_packed(t_ref, slots, spot_ref, slot_fine, sf, (m0, m1, m2, m3))


BIG = (NQ, NB, LN)
TAB = (NQ, FA, LN)
MSG = (PK, LN)


def call(kernel, name, outs, scratch, args, size=4, space=pltpu.VMEM, limit=24):
    return pl.pallas_call(
        kernel,
        name=name,
        out_shape=[jax.ShapeDtypeStruct(s, d) for s, d in outs],
        in_specs=[pl.BlockSpec(memory_space=space)] * len(args),
        out_specs=[pl.BlockSpec(memory_space=pltpu.VMEM)] * len(outs),
        scratch_shapes=[pltpu.VMEM(*x) if isinstance(x, tuple) else x for x in scratch],
        compiler_params=pltpu.CompilerParams(vmem_limit_bytes=limit << 20),
        cost_estimate=pl.CostEstimate(flops=50_000_000, bytes_accessed=size << 20, transcendentals=0),
    )(*args)


def partners(devices):
    def pairing(step, start, ends):
        pairs = []
        for i in range(devices):
            j = i - start
            t = start + (j ^ step) if j >= 0 else -1
            if t < start or t >= devices:
                t = ends(i)
            pairs.append((i, t))
        return pairs
    return (
        pairing(1, 0, lambda i: i),
        pairing(1, 1, lambda i: devices - 1 - i),
        pairing(2, 0, lambda i: i),
        pairing(2, 2, lambda i: i ^ 1),
    )


def shards(dofs, star, flux_minus, flux_plus, cohesion, stiff, face_proj, lift, rotate, cluster,
           neighbor, neigh_face, orient, send_elem, send_face):
    devices = lax.axis_size("dom")
    pairings = partners(devices)

    def exchange(messages):
        got = [None] * 4
        for k in (2, 3, 1, 0):
            got[k] = lax.ppermute(messages[k], "dom", pairings[k])
        return got

    i32 = jnp.int32
    args = [
        jnp.transpose(dofs, (1, 0, 2)), jnp.transpose(star, (1, 2, 0, 3)),
        jnp.transpose(flux_minus, (1, 2, 0, 3)), jnp.transpose(flux_plus, (1, 2, 0, 3)),
        cohesion.reshape(1, LN), stiff, jnp.transpose(face_proj, (1, 0, 2)),
        jnp.transpose(lift, (2, 0, 1)), rotate, cluster.reshape(1, LN), neighbor, neigh_face,
        orient, send_elem, send_face]
    scratch = [pltpu.VMEM(args[n].shape, args[n].dtype) for n in (1, 5, 6, 13, 14, 10)]
    outs = call(
        first_kernel, "first",
        [((NQ, NQ, 3, LN), F32), ((2 * NB, 3 * NB), BF16), ((2 * FA, NB), BF16),
         ((ORDER,) + BIG, F32), (BIG, F32), (TAB, F32)] + [(MSG, F32)] * 4
        + [((1, LN), i32), ((1, LN), i32), ((4, LN), i32), (args[2].shape, F32),
           (args[3].shape, F32), ((4, LN), i32), ((4, LN), i32), ((1, LN), F32), ((1, LN), i32),
           (args[7].shape, F32), (args[8].shape, F32)],
        scratch + [pltpu.SemaphoreType.DMA((15,))],
        [pltpu.with_memory_space_constraint(a, pltpu.HBM) for a in args], space=pltpu.HBM)
    s_mat, w2, p2, series, pred, table = outs[:6]
    got = exchange(outs[6:10])
    se, sf, nb, fm, fp, nf, turn_code, coh, fine, lift, rotate = outs[10:]
    l2, lr2, order, spot, packed, slot_spot, slot_fine, slot_flux = call(
        lift_kernel, "lifts",
        [((2 * NB, FA), BF16), ((2 * NB, 3 * FA), BF16), ((8, LN), i32), ((2, 8, LN), i32),
         ((PAIRS, 2 * PAIRS, 3, LN), F32), ((2, 8, LN), i32), ((8, LN), i32), ((NQ, NQ, LN), F32)],
        [((NQ, NQ, 8, LN), F32)],
        [lift, rotate, s_mat, fine, se, nb, fp])
    acc = sums = piece = None
    state = series[0]
    half = ((PAIRS, NB, LN), F32)
    for sub in range(RATE):
        last = sub == RATE - 1
        u, near, *coming = call(
            functools.partial(local_kernel, sub), "local",
            [(BIG, F32), (BIG, F32)] + ([] if last else [(BIG, F32), ((NQ, FR, LN), F32)]),
            [(TAB, F32)] + ([(BIG, F32), (TAB, F32)] if sub else []),
            [state, s_mat, w2, p2, fm, l2, fp, lr2, nb, nf, turn_code, series, se, sf, fine, spot]
            + ([sums, piece] if sub else [pred, table]), 8)
        if sub == 1:
            coarse = call(
                coarse_kernel, "coarse_own", [(BIG, F32)], [(BIG, F32), (TAB, F32)],
                [series, s_mat, w2, p2, fm, l2, outs[3]], 8)[0]
        common = [got[2], got[3], got[1], got[0], slot_flux, lr2, nb, turn_code, u, near]
        if last:
            out = call(
                last_kernel, "last", [(BIG, F32)], [(BIG, F32)],
                common + [acc, coarse, coh, fine])[0]
            return jnp.transpose(out, (1, 0, 2))
        piece, slots = coming
        outs = call(
            functools.partial(join_kernel, acc is None), "join",
            [(BIG, F32), (BIG, F32), half] + [(MSG, F32)] * 4,
            [(BIG, F32), ((2, 2 * PAIRS, NB, LN), F32), ((PAIRS, FA, LN), F32)],
            common + [near if acc is None else acc, coh, fine, state, packed, w2, p2, slots, sf,
                      order, slot_spot, slot_fine])
        state, acc, sums = outs[:3]
        got = exchange(outs[3:])


def solution(mesh):
    placed = (
        P(None, None, "dom"),
        P(None, None, None, "dom"),
        P(None, None, None, "dom"),
        P(None, None, None, "dom"),
        P("dom"),
        P(),
        P(),
        P(),
        P(),
        P("dom"),
        P(None, "dom"),
        P(None, "dom"),
        P(None, "dom"),
        P(None, "dom"),
        P(None, "dom"),
    )
    return jax.shard_map(
        shards, mesh=mesh, in_specs=placed, out_specs=P(None, None, "dom"), check_vma=False)
```

```python
import functools
import math

import jax
import jax.numpy as jnp
from jax import lax
from jax.experimental import pallas as pl
from jax.experimental.pallas import tpu as pltpu
from jax.sharding import PartitionSpec as P

ORDER = 6
RATE = 4
F32 = jnp.float32
BF16 = jnp.bfloat16
NB = 56
NQ = 9
FR = 24
FA = 4 * FR
LN = 128
PK = 56
PAIRS = 5


def dot(a, b):
    return jnp.dot(a, b, preferred_element_type=F32)


def exact(a, b):
    return jnp.dot(a, b, preferred_element_type=F32, precision=lax.Precision.HIGHEST)


def split(x):
    hi = x.astype(BF16)
    return hi, (x - hi.astype(F32)).astype(BF16)


def two_rows(w):
    hi, lo = split(w)
    return jnp.concatenate([hi.astype(F32), lo.astype(F32)], axis=0).astype(BF16)


def times(w2, rhs, rows):
    hi, lo = split(rhs)
    both = dot(w2, hi)
    return both[:rows] + both[rows:] + dot(w2[:rows], lo)


def side_by_side(w2, halves):
    out = dot(w2, halves)
    return out[:NB, :LN] + out[NB:, :LN] + out[:NB, LN:]


def lift_times(w2, rhs):
    return side_by_side(w2, jnp.concatenate(split(rhs), axis=1))


def star_rows(s_ref, q, which, values):
    total = s_ref[q, 0, which:which + 1, :] * values(0)
    for p in range(1, NQ):
        total = total + s_ref[q, p, which:which + 1, :] * values(p)
    return total


def operator(x_ref, s_ref, w2):
    out = []
    for q in range(NQ):
        stacked = jnp.concatenate(
            [star_rows(s_ref, q, c, lambda p: x_ref[p]) for c in range(3)], axis=0)
        out.append(lift_times(w2, stacked))
    return out


def packed_operator(y_ref, s_ref, w2):
    out = []
    for j in range(PAIRS):
        parts = []
        for c in range(3):
            total = s_ref[j, 0, c:c + 1, :] * y_ref[0]
            for m in range(1, 2 * PAIRS):
                total = total + s_ref[j, m, c:c + 1, :] * y_ref[m]
            parts.append(total)
        out.append(lift_times(w2, jnp.concatenate(parts, axis=0)))
    return out


def both_ways(y_ref, j, rows):
    y_ref[2 * j] = rows
    y_ref[2 * j + 1] = pltpu.roll(rows, LN // 2, 1)


def traces(x_ref, p2, t_ref):
    for q in range(NQ):
        t_ref[q] = times(p2, x_ref[q], FA)


def lanes(shape):
    return lax.broadcasted_iota(jnp.int32, shape, len(shape) - 1)


def pick(rows, index):
    return jnp.take_along_axis(rows, index, axis=1, mode="promise_in_bounds")


def send(t_ref, se_ref, sf_ref, out_refs):
    elem = jnp.broadcast_to(se_ref[...], (FR, LN))
    face = jnp.broadcast_to(sf_ref[...], (FR, LN))
    rows = []
    for q in range(NQ):
        got = pick(t_ref[q, 0:FR], elem)
        for f in range(1, 4):
            got = jnp.where(face == f, pick(t_ref[q, f * FR:(f + 1) * FR], elem), got)
        rows.append(got)
    rows.append(jnp.zeros((4 * PK - NQ * FR, LN), F32))
    table = jnp.concatenate(rows, axis=0)
    group = lanes((PK, LN)) // 32
    for k in range(4):
        message = None
        for g in range(4):
            part = table[g * PK:(g + 1) * PK]
            if g != k:
                part = pltpu.roll(part, ((g - k) * 32) % LN, 1)
            message = part if message is None else jnp.where(group == g, part, message)
        out_refs[k][...] = message


def unpack(in_refs):
    group = lanes((PK, LN)) // 32
    parts = []
    for g in range(4):
        rows = None
        for k in range(4):
            part = in_refs[k][...]
            if g != k:
                part = pltpu.roll(part, ((k - g) * 32) % LN, 1)
            rows = part if rows is None else jnp.where(group == k, part, rows)
        parts.append(rows)
    return jnp.concatenate(parts, axis=0)


def local_pick(t_ref, nb_ref, nf_ref, out_ref):
    for f in range(4):
        where = jnp.broadcast_to(nb_ref[f:f + 1, :], (FR, LN))
        face = jnp.broadcast_to(nf_ref[f:f + 1, :], (FR, LN))
        elem = jnp.minimum(where, LN - 1)
        face = jnp.where(where < LN, face, 4)
        for q in range(NQ):
            got = jnp.zeros((FR, LN), F32)
            for g in range(4):
                got = jnp.where(face == g, pick(t_ref[q, g * FR:(g + 1) * FR], elem), got)
            out_ref[q, f * FR:(f + 1) * FR] = got


def ghost_pick(table, nb_ref, local_ref, out_ref):
    for f in range(4):
        where = jnp.broadcast_to(nb_ref[f:f + 1, :], (FR, LN))
        slot = jnp.clip(where - LN, 0, LN - 1)
        ghost = (where >= LN) & (where < 2 * LN)
        for q in range(NQ):
            got = pick(table[q * FR:(q + 1) * FR], slot)
            out_ref[q, f * FR:(f + 1) * FR] = jnp.where(
                ghost, got, local_ref[q, f * FR:(f + 1) * FR])


def flux_rows(f_ref, q, t_ref):
    return jnp.concatenate(
        [star_rows(f_ref, q, f, lambda p: t_ref[p, f * FR:(f + 1) * FR]) for f in range(4)],
        axis=0)


def own_term(f_ref, t_ref, l2, q):
    return lift_times(l2, flux_rows(f_ref, q, t_ref))


def orient_masks(or_ref):
    codes = jnp.concatenate(
        [jnp.broadcast_to(or_ref[f:f + 1, :], (FR, LN)) for f in range(4)], axis=0)
    masks = [(codes == k).astype(F32).astype(BF16) for k in range(3)]
    return [jnp.concatenate([m, m], axis=1) for m in masks]


def plastic(u_ref, cohesion):
    s = [u_ref[q, 0:1, :] for q in range(6)]
    mean = (s[0] + s[1] + s[2]) / 3.0
    dx, dy, dz = s[0] - mean, s[1] - mean, s[2] - mean
    second = 0.5 * (dx * dx + dy * dy + dz * dz) + s[3] * s[3] + s[4] * s[4] + s[5] * s[5]
    factor = cohesion / jnp.maximum(jnp.sqrt(second), cohesion)
    pressure = (u_ref[0] + u_ref[1] + u_ref[2]) / 3.0
    out = [pressure + factor * (u_ref[i] - pressure) for i in range(3)]
    out += [factor * u_ref[i] for i in range(3, 6)]
    return out + [u_ref[i] for i in range(6, NQ)]


def place(width, offset, rows):
    r = lax.broadcasted_iota(jnp.int32, (rows, width), 0)
    return (lanes((rows, width)) == r + offset).astype(F32)


def weigh(series, end, begin, q):
    total = None
    for k in range(ORDER):
        term = (end ** (k + 1) - begin ** (k + 1)) / math.factorial(k + 1) * series[k, q]
        total = term if total is None else total + term
    return total


def slot_row(table, one_up, two_up):
    values = table[...].astype(F32).astype(BF16)
    total = None
    for k, (here, there, up) in enumerate(
            ((2, 1, one_up), (1, 2, one_up), (3, 0, two_up), (0, 3, two_up))):
        spread = dot(values, place(LN, 32 * k, 32).astype(BF16))
        row = jnp.where(up, spread[here:here + 1], spread[there:there + 1])
        total = row if total is None else total + row
    return total.astype(jnp.int32)


def first_kernel(*refs):
    ins, outs, scratch = refs[:15], refs[15:36], refs[36:]
    (s_out, w2_out, p2_out, series, piece, t_out, m0, m1, m2, m3, se_out, sf_out, nb_out) = outs[:13]
    fm_out, fp_out, nf_out, or_out, coh_out, fine_out, lift_out, turn_out = outs[13:]
    star, stiff, proj, se, sf, nb, sems = scratch
    places = (series.at[0], star, fm_out, fp_out, coh_out, stiff, proj, lift_out, turn_out, fine_out, nb,
              nf_out, or_out, se, sf)
    copies = [pltpu.make_async_copy(a, b, sems.at[n]) for n, (a, b) in enumerate(zip(ins, places))]
    early = (5, 1, 0, 6, 13, 14)
    rest = [n for n in range(15) if n not in early]
    for n in early:
        copies[n].start()
    for n in rest:
        copies[n].start()
    copies[5].wait()
    minus = [0.5 * (jnp.transpose(stiff[c]) - stiff[c]) for c in range(3)]
    w2_out[...] = two_rows(jnp.concatenate(minus, axis=1))
    copies[1].wait()
    for q in range(NQ):
        for p in range(q + 1):
            s_out[q, p] = 0.5 * (star[q, p] + star[p, q])
            if p != q:
                s_out[p, q] = s_out[q, p]
    copies[0].wait()
    for q in range(NQ):
        piece[q] = series[0, q] * (1.0 / RATE)

    for k in range(ORDER - 1):
        weight = (1.0 / RATE) ** (k + 2) / math.factorial(k + 2)
        rows = operator(series.at[k], s_out, w2_out[...])
        for q in range(NQ):
            series[k + 1, q] = rows[q]
            piece[q] += weight * rows[q]
    for n in (6, 13, 14):
        copies[n].wait()
    faces = []
    for f in range(4):
        faces += [proj[:, f, :], jnp.zeros((FR - proj.shape[0], NB), F32)]
    p2_out[...] = two_rows(jnp.concatenate(faces, axis=0))
    me = lax.axis_index("dom")
    one_up = lax.rem(me, 2) == 0
    two_up = lax.rem(me, 4) < 2
    se_out[...] = slot_row(se, one_up, two_up)
    sf_out[...] = slot_row(sf, one_up, two_up)
    traces(piece, p2_out[...], t_out)
    send(t_out, se_out, sf_out, (m0, m1, m2, m3))
    for n in rest:
        copies[n].wait()
    two = jnp.where(one_up, 0, 1)
    three = jnp.where(two_up, 2, 3)
    ghost = nb[...] - LN
    block, slot = ghost >> 5, ghost & 31
    place_of = jnp.where(
        block == 2, two, jnp.where(block == 1, 1 - two, jnp.where(block == 3, three, 5 - three)))
    nb_out[...] = jnp.where((ghost >= 0) & (ghost < LN), LN + place_of * 32 + slot, nb[...])


def lift_kernel(lift, rotate, s_ref, fine_ref, l2_out, lr2_out, order_out, spot_out, pack_out, rows):
    is_fine = jnp.broadcast_to(fine_ref[...], (LN, LN))
    down = lax.broadcasted_iota(jnp.int32, (LN, LN), 0)
    across = lanes((LN, LN))
    ahead = (down < across).astype(F32).astype(BF16)
    spot = dot(is_fine.astype(F32).astype(BF16), ahead)
    own_spot = jnp.transpose(spot).astype(jnp.int32)
    own_fine = jnp.transpose(is_fine.astype(F32)) > 0.5
    chosen = own_fine & (own_spot == across % (LN // 2))
    order = dot(across.astype(F32).astype(BF16), chosen.astype(F32).astype(BF16)).astype(jnp.int32)
    order_out[...] = order[0:8]
    low = jnp.minimum(spot.astype(jnp.int32), LN // 2 - 1)
    spot_out[0] = low[0:8]
    spot_out[1] = low[0:8] + LN // 2
    order = order[0:8]
    for q in range(NQ):
        for p in range(q + 1):
            got = pick(jnp.concatenate([s_ref[q, p], jnp.zeros((5, LN), F32)], axis=0), order)
            rows[q, p] = got
            rows[p, q] = got
    left = lanes((3, LN)) < LN // 2

    def entry(q, p):
        return rows[q, p, 0:3] if q < NQ and p < NQ else jnp.zeros((3, LN), F32)

    for j in range(PAIRS):
        for i in range(PAIRS):
            a, b = 2 * j, 2 * i
            pack_out[j, b] = jnp.where(left, entry(a, b), entry(a + 1, b + 1))
            pack_out[j, b + 1] = jnp.where(left, entry(a, b + 1), entry(a + 1, b))
    gap = jnp.zeros((FR - lift.shape[0], NB), F32)
    own, turned = [], [[] for _ in range(3)]
    turns = [jnp.transpose(rotate[k]) for k in range(3)]
    for f in range(4):
        flipped = lift[:, f, :]
        own += [flipped, gap]
        for k in range(3):
            turned[k] += [exact(turns[k], flipped), gap]
    l2_out[...] = two_rows(jnp.transpose(jnp.concatenate(own, axis=0)))
    lr2_out[...] = two_rows(jnp.transpose(jnp.concatenate(turned[0] + turned[1] + turned[2], axis=0)))


def coarse_kernel(series, s_ref, w2, p2, fm_ref, l2, after, u_out, full, t_full):
    del after
    for q in range(NQ):
        full[q] = weigh(series, 1.0, 0.0, q)
    traces(full, p2[...], t_full)
    rows = operator(full, s_ref, w2[...])
    for q in range(NQ):
        u_out[q] = series[0, q] + rows[q] - own_term(fm_ref, t_full, l2[...], q)


def local_kernel(sub, q_ref, pred, t_ref, s_ref, w2, fm_ref, l2, nb_ref, nf_ref, series, u_out,
                 n_out, *next_out):
    rows = operator(pred, s_ref, w2[...])
    for q in range(NQ):
        u_out[q] = q_ref[q] + rows[q] - own_term(fm_ref, t_ref, l2[...], q)
    local_pick(t_ref, nb_ref, nf_ref, n_out)
    if next_out:
        for q in range(NQ):
            next_out[0][q] = weigh(series, (sub + 2) / RATE, (sub + 1) / RATE, q)


def join_kernel(last, *refs):
    (g3, g2, g1, g0, q_ref, u_ref, nl_ref, nacc_ref, fp_ref, lr2, nb_ref, or_ref, coh, fine_ref,
     pack_ref, w2, p2, piece, se, sf, order_ref, spot_ref) = refs[:22]
    table = unpack((g0, g1, g2, g3))
    masks = orient_masks(or_ref)
    fine = fine_ref[...] == 1
    if last:
        uc_ref, out, n_ref, work = refs[22:]
    else:
        q_out, n_out, pred, t_out, m0, m1, m2, m3, n_ref, work, series, sums = refs[22:]

    def face_terms(values):
        for q in range(NQ):
            halves = jnp.concatenate(split(flux_rows(fp_ref, q, n_ref)), axis=1)
            sub = side_by_side(lr2[...], jnp.concatenate([halves * m for m in masks], axis=0))
            work[q] = values(q) - sub

    ghost_pick(table, nb_ref, nl_ref, n_ref)
    if last:
        for q in range(NQ):
            n_ref[q] = jnp.where(fine, n_ref[q], nacc_ref[q] + n_ref[q])
        face_terms(lambda q: jnp.where(fine, u_ref[q], uc_ref[q]))
        after = plastic(work, coh[...])
        for q in range(NQ):
            out[q] = after[q]
        return
    face_terms(lambda q: u_ref[q])
    after = plastic(work, coh[...])
    for q in range(NQ):
        n_out[q] = nacc_ref[q] + n_ref[q] if nacc_ref is not None else n_ref[q]
        x = jnp.where(fine, after[q], q_ref[q])
        q_out[q] = x
    order = jnp.broadcast_to(order_ref[0:1, :], (NB, LN))
    left = lanes((NB, LN)) < LN // 2
    for j in range(PAIRS):
        rows = pick(q_out[2 * j], order)
        other = pick(q_out[2 * j + 1], order) if 2 * j + 1 < NQ else jnp.zeros((NB, LN), F32)
        rows = jnp.where(left, rows, other)
        both_ways(series.at[0], j, rows)
        sums[j] = rows * (1.0 / RATE)

    for k in range(ORDER - 1):
        weight = (1.0 / RATE) ** (k + 2) / math.factorial(k + 2)
        rows = packed_operator(series.at[k % 2], pack_ref, w2[...])
        for j in range(PAIRS):
            if k < ORDER - 2:
                both_ways(series.at[(k + 1) % 2], j, rows[j])
            sums[j] += weight * rows[j]
    for q in range(NQ):
        spot = jnp.broadcast_to(spot_ref[q % 2, 0:1, :], (NB, LN))
        pred[q] = jnp.where(fine, pick(sums[q // 2], spot), piece[q])
    traces(pred, p2[...], t_out)
    send(t_out, se, sf, (m0, m1, m2, m3))


BIG = (NQ, NB, LN)
TAB = (NQ, FA, LN)
MSG = (PK, LN)


def call(kernel, name, outs, scratch, args, size=4, space=pltpu.VMEM, limit=24):
    return pl.pallas_call(
        kernel,
        name=name,
        out_shape=[jax.ShapeDtypeStruct(s, d) for s, d in outs],
        in_specs=[pl.BlockSpec(memory_space=space)] * len(args),
        out_specs=[pl.BlockSpec(memory_space=pltpu.VMEM)] * len(outs),
        scratch_shapes=[pltpu.VMEM(*x) if isinstance(x, tuple) else x for x in scratch],
        compiler_params=pltpu.CompilerParams(vmem_limit_bytes=limit << 20),
        cost_estimate=pl.CostEstimate(flops=50_000_000, bytes_accessed=size << 20, transcendentals=0),
    )(*args)


def partners(devices):
    def pairing(step, start, ends):
        pairs = []
        for i in range(devices):
            j = i - start
            t = start + (j ^ step) if j >= 0 else -1
            if t < start or t >= devices:
                t = ends(i)
            pairs.append((i, t))
        return pairs
    return (
        pairing(1, 0, lambda i: i),
        pairing(1, 1, lambda i: devices - 1 - i),
        pairing(2, 0, lambda i: i),
        pairing(2, 2, lambda i: i ^ 1),
    )


def shards(dofs, star, flux_minus, flux_plus, cohesion, stiff, face_proj, lift, rotate, cluster,
           neighbor, neigh_face, orient, send_elem, send_face):
    devices = lax.axis_size("dom")
    pairings = partners(devices)

    def exchange(messages):
        got = [None] * 4
        for k in (2, 3, 1, 0):
            got[k] = lax.ppermute(messages[k], "dom", pairings[k])
        return got

    i32 = jnp.int32
    args = [
        jnp.transpose(dofs, (1, 0, 2)), jnp.transpose(star, (1, 2, 0, 3)),
        jnp.transpose(flux_minus, (1, 2, 0, 3)), jnp.transpose(flux_plus, (1, 2, 0, 3)),
        cohesion.reshape(1, LN), stiff, jnp.transpose(face_proj, (1, 0, 2)),
        jnp.transpose(lift, (2, 0, 1)), rotate, cluster.reshape(1, LN), neighbor, neigh_face,
        orient, send_elem, send_face]
    scratch = [pltpu.VMEM(args[n].shape, args[n].dtype) for n in (1, 5, 6, 13, 14, 10)]
    outs = call(
        first_kernel, "first",
        [((NQ, NQ, 3, LN), F32), ((2 * NB, 3 * NB), BF16), ((2 * FA, NB), BF16),
         ((ORDER,) + BIG, F32), (BIG, F32), (TAB, F32)] + [(MSG, F32)] * 4
        + [((1, LN), i32), ((1, LN), i32), ((4, LN), i32), (args[2].shape, F32),
           (args[3].shape, F32), ((4, LN), i32), ((4, LN), i32), ((1, LN), F32), ((1, LN), i32),
           (args[7].shape, F32), (args[8].shape, F32)],
        scratch + [pltpu.SemaphoreType.DMA((15,))],
        [pltpu.with_memory_space_constraint(a, pltpu.HBM) for a in args], space=pltpu.HBM)
    s_mat, w2, p2, series, pred, table = outs[:6]
    got = exchange(outs[6:10])
    se, sf, nb, fm, fp, nf, turn_code, coh, fine, lift, rotate = outs[10:]
    l2, lr2, order, spot, pack = call(
        lift_kernel, "lifts",
        [((2 * NB, FA), BF16), ((2 * NB, 3 * FA), BF16), ((8, LN), i32), ((2, 8, LN), i32),
         ((PAIRS, 2 * PAIRS, 3, LN), F32)],
        [((NQ, NQ, 8, LN), F32)],
        [lift, rotate, s_mat, fine])
    total = coarse = None
    state = series[0]
    for sub in range(RATE):
        last = sub == RATE - 1
        u, near, *piece = call(
            functools.partial(local_kernel, sub), "local",
            [(BIG, F32), (TAB, F32)] + ([] if last else [(BIG, F32)]), [],
            [state, pred, table, s_mat, w2, fm, l2, nb, nf, series])
        if sub == 1:
            coarse = call(
                coarse_kernel, "coarse_own", [(BIG, F32)], [(BIG, F32), (TAB, F32)],
                [series, s_mat, w2, p2, fm, l2, outs[4]], 8)[0]
        common = [got[3], got[2], got[1], got[0], state, u, near, total if total is not None else near, fp, lr2, nb, turn_code,
                  coh, fine, pack, w2, p2]
        if last:
            out = call(
                functools.partial(join_kernel, True), "last", [(BIG, F32)],
                [(TAB, F32), (BIG, F32)],
                common + [near, se, sf, order, spot, coarse])[0]
            return jnp.transpose(out, (1, 0, 2))
        first = total is None

        def kernel(*refs, first=first):
            refs = list(refs)
            if first:
                refs[7] = None
            join_kernel(False, *refs)

        outs = call(
            kernel, "join",
            [(BIG, F32), (TAB, F32), (BIG, F32), (TAB, F32)] + [(MSG, F32)] * 4,
            [(TAB, F32), (BIG, F32), ((2, 2 * PAIRS, NB, LN), F32), ((PAIRS, NB, LN), F32)],
            common + [piece[0], se, sf, order, spot])
        state, total, pred, table = outs[:4]
        got = exchange(outs[4:])


def solution(mesh):
    placed = (
        P(None, None, "dom"),
        P(None, None, None, "dom"),
        P(None, None, None, "dom"),
        P(None, None, None, "dom"),
        P("dom"),
        P(),
        P(),
        P(),
        P(),
        P("dom"),
        P(None, "dom"),
        P(None, "dom"),
        P(None, "dom"),
        P(None, "dom"),
        P(None, "dom"),
    )
    return jax.shard_map(
        shards, mesh=mesh, in_specs=placed, out_specs=P(None, None, "dom"), check_vma=False)
```

```python
import functools
import math

import jax
import jax.numpy as jnp
from jax import lax
from jax.experimental import pallas as pl
from jax.experimental.pallas import tpu as pltpu
from jax.sharding import PartitionSpec as P

ORDER = 6
RATE = 4
F32 = jnp.float32
BF16 = jnp.bfloat16
NB = 56
NQ = 9
FR = 24
FA = 4 * FR
LN = 128
PK = 56
PAIRS = 5


def dot(a, b):
    return jnp.dot(a, b, preferred_element_type=F32)


def exact(a, b):
    return jnp.dot(a, b, preferred_element_type=F32, precision=lax.Precision.HIGHEST)


def split(x):
    hi = x.astype(BF16)
    return hi, (x - hi.astype(F32)).astype(BF16)


def two_rows(w):
    hi, lo = split(w)
    return jnp.concatenate([hi.astype(F32), lo.astype(F32)], axis=0).astype(BF16)


def times(w2, rhs, rows):
    hi, lo = split(rhs)
    both = dot(w2, hi)
    return both[:rows] + both[rows:] + dot(w2[:rows], lo)


def side_by_side(w2, halves):
    out = dot(w2, halves)
    return out[:NB, :LN] + out[NB:, :LN] + out[:NB, LN:]


def lift_times(w2, rhs):
    return side_by_side(w2, jnp.concatenate(split(rhs), axis=1))


def star_rows(s_ref, q, which, values):
    total = s_ref[q, 0, which:which + 1, :] * values(0)
    for p in range(1, NQ):
        total = total + s_ref[q, p, which:which + 1, :] * values(p)
    return total


def operator(x_ref, s_ref, w2):
    out = []
    for q in range(NQ):
        stacked = jnp.concatenate(
            [star_rows(s_ref, q, c, lambda p: x_ref[p]) for c in range(3)], axis=0)
        out.append(lift_times(w2, stacked))
    return out


def packed_operator(y_ref, s_ref, w2):
    out = []
    for j in range(PAIRS):
        parts = []
        for c in range(3):
            total = s_ref[j, 0, c:c + 1, :] * y_ref[0]
            for m in range(1, 2 * PAIRS):
                total = total + s_ref[j, m, c:c + 1, :] * y_ref[m]
            parts.append(total)
        out.append(lift_times(w2, jnp.concatenate(parts, axis=0)))
    return out


def both_ways(y_ref, j, rows):
    y_ref[2 * j] = rows
    y_ref[2 * j + 1] = pltpu.roll(rows, LN // 2, 1)


def traces(x_ref, p2, t_ref):
    for q in range(NQ):
        t_ref[q] = times(p2, x_ref[q], FA)


def lanes(shape):
    return lax.broadcasted_iota(jnp.int32, shape, len(shape) - 1)


def pick(rows, index):
    return jnp.take_along_axis(rows, index, axis=1, mode="promise_in_bounds")


def chosen_face(face, rows):
    got = rows(0)
    for f in range(1, 4):
        got = jnp.where(face == f, rows(f), got)
    return got


def pack(rows, out_refs):
    table = jnp.concatenate(rows + [jnp.zeros((4 * PK - NQ * FR, LN), F32)], axis=0)
    group = lanes((PK, LN)) // 32
    for k in range(4):
        message = None
        for g in range(4):
            part = table[g * PK:(g + 1) * PK]
            if g != k:
                part = pltpu.roll(part, ((g - k) * 32) % LN, 1)
            message = part if message is None else jnp.where(group == g, part, message)
        out_refs[k][...] = message


def send(t_ref, se_ref, sf_ref, out_refs):
    elem = jnp.broadcast_to(se_ref[...], (FR, LN))
    face = jnp.broadcast_to(sf_ref[...], (FR, LN))
    pack([chosen_face(face, lambda f: pick(t_ref[q, f * FR:(f + 1) * FR], elem))
          for q in range(NQ)], out_refs)


def send_packed(t_ref, coarse_ref, spot_ref, slot_fine, sf_ref, out_refs):
    face = jnp.broadcast_to(sf_ref[...], (FR, LN))
    is_fine = jnp.broadcast_to(slot_fine[0:1, :], (FR, LN)) == 1
    rows = []
    for q in range(NQ):
        spot = jnp.broadcast_to(spot_ref[q % 2, 0:1, :], (FR, LN))
        got = chosen_face(face, lambda f: pick(t_ref[q // 2, f * FR:(f + 1) * FR], spot))
        rows.append(jnp.where(is_fine, got, coarse_ref[q]))
    pack(rows, out_refs)


def unpack(in_refs):
    group = lanes((PK, LN)) // 32
    parts = []
    for g in range(4):
        rows = None
        for k in range(4):
            part = in_refs[k][...]
            if g != k:
                part = pltpu.roll(part, ((k - g) * 32) % LN, 1)
            rows = part if rows is None else jnp.where(group == k, part, rows)
        parts.append(rows)
    return jnp.concatenate(parts, axis=0)


def local_pick(t_ref, nb_ref, nf_ref, out_ref):
    for f in range(4):
        where = jnp.broadcast_to(nb_ref[f:f + 1, :], (FR, LN))
        face = jnp.broadcast_to(nf_ref[f:f + 1, :], (FR, LN))
        elem = jnp.minimum(where, LN - 1)
        face = jnp.where(where < LN, face, 4)
        for q in range(NQ):
            got = jnp.zeros((FR, LN), F32)
            for g in range(4):
                got = jnp.where(face == g, pick(t_ref[q, g * FR:(g + 1) * FR], elem), got)
            out_ref[q, f * FR:(f + 1) * FR] = got


def ghost_rows(values, nb_ref):
    out = []
    for f in range(4):
        where = jnp.broadcast_to(nb_ref[f:f + 1, :], (FR, LN))
        slot = jnp.clip(where - LN, 0, LN - 1)
        ghost = (where >= LN) & (where < 2 * LN)
        out.append(jnp.where(ghost, pick(values, slot), 0.0))
    return jnp.concatenate(out, axis=0)


def turned_lift(lr2, masks, rows):
    halves = jnp.concatenate(split(rows), axis=1)
    return side_by_side(lr2, jnp.concatenate([halves * m for m in masks], axis=0))


def flux_rows(f_ref, q, t_ref):
    return jnp.concatenate(
        [star_rows(f_ref, q, f, lambda p: t_ref[p, f * FR:(f + 1) * FR]) for f in range(4)],
        axis=0)


def own_term(f_ref, t_ref, l2, q):
    return lift_times(l2, flux_rows(f_ref, q, t_ref))


def orient_masks(or_ref):
    codes = jnp.concatenate(
        [jnp.broadcast_to(or_ref[f:f + 1, :], (FR, LN)) for f in range(4)], axis=0)
    masks = [(codes == k).astype(F32).astype(BF16) for k in range(3)]
    return [jnp.concatenate([m, m], axis=1) for m in masks]


def plastic(u_ref, cohesion):
    s = [u_ref[q, 0:1, :] for q in range(6)]
    mean = (s[0] + s[1] + s[2]) / 3.0
    dx, dy, dz = s[0] - mean, s[1] - mean, s[2] - mean
    second = 0.5 * (dx * dx + dy * dy + dz * dz) + s[3] * s[3] + s[4] * s[4] + s[5] * s[5]
    factor = cohesion / jnp.maximum(jnp.sqrt(second), cohesion)
    pressure = (u_ref[0] + u_ref[1] + u_ref[2]) / 3.0
    out = [pressure + factor * (u_ref[i] - pressure) for i in range(3)]
    out += [factor * u_ref[i] for i in range(3, 6)]
    return out + [u_ref[i] for i in range(6, NQ)]


def place(width, offset, rows):
    r = lax.broadcasted_iota(jnp.int32, (rows, width), 0)
    return (lanes((rows, width)) == r + offset).astype(F32)


def weigh(series, end, begin, q):
    total = None
    for k in range(ORDER):
        term = (end ** (k + 1) - begin ** (k + 1)) / math.factorial(k + 1) * series[k, q]
        total = term if total is None else total + term
    return total


def slot_row(table, one_up, two_up):
    values = table[...].astype(F32).astype(BF16)
    total = None
    for k, (here, there, up) in enumerate(
            ((2, 1, one_up), (1, 2, one_up), (3, 0, two_up), (0, 3, two_up))):
        spread = dot(values, place(LN, 32 * k, 32).astype(BF16))
        row = jnp.where(up, spread[here:here + 1], spread[there:there + 1])
        total = row if total is None else total + row
    return total.astype(jnp.int32)


def first_kernel(*refs):
    ins, outs, scratch = refs[:15], refs[15:36], refs[36:]
    (s_out, w2_out, p2_out, series, piece, t_out, m0, m1, m2, m3, se_out, sf_out, nb_out) = outs[:13]
    fm_out, fp_out, nf_out, or_out, coh_out, fine_out, lift_out, turn_out = outs[13:]
    star, stiff, proj, se, sf, nb, sems = scratch
    places = (series.at[0], star, fm_out, fp_out, coh_out, stiff, proj, lift_out, turn_out, fine_out, nb,
              nf_out, or_out, se, sf)
    copies = [pltpu.make_async_copy(a, b, sems.at[n]) for n, (a, b) in enumerate(zip(ins, places))]
    early = (5, 1, 0, 6, 13, 14)
    rest = [n for n in range(15) if n not in early]
    for n in early:
        copies[n].start()
    for n in rest:
        copies[n].start()
    copies[5].wait()
    minus = [0.5 * (jnp.transpose(stiff[c]) - stiff[c]) for c in range(3)]
    w2_out[...] = two_rows(jnp.concatenate(minus, axis=1))
    copies[1].wait()
    for q in range(NQ):
        for p in range(q + 1):
            s_out[q, p] = 0.5 * (star[q, p] + star[p, q])
            if p != q:
                s_out[p, q] = s_out[q, p]
    copies[0].wait()
    for q in range(NQ):
        piece[q] = series[0, q] * (1.0 / RATE)

    for k in range(ORDER - 1):
        weight = (1.0 / RATE) ** (k + 2) / math.factorial(k + 2)
        rows = operator(series.at[k], s_out, w2_out[...])
        for q in range(NQ):
            series[k + 1, q] = rows[q]
            piece[q] += weight * rows[q]
    for n in (6, 13, 14):
        copies[n].wait()
    faces = []
    for f in range(4):
        faces += [proj[:, f, :], jnp.zeros((FR - proj.shape[0], NB), F32)]
    p2_out[...] = two_rows(jnp.concatenate(faces, axis=0))
    me = lax.axis_index("dom")
    one_up = lax.rem(me, 2) == 0
    two_up = lax.rem(me, 4) < 2
    se_out[...] = slot_row(se, one_up, two_up)
    sf_out[...] = slot_row(sf, one_up, two_up)
    traces(piece, p2_out[...], t_out)
    send(t_out, se_out, sf_out, (m0, m1, m2, m3))
    for n in rest:
        copies[n].wait()
    two = jnp.where(one_up, 0, 1)
    three = jnp.where(two_up, 2, 3)
    ghost = nb[...] - LN
    block, slot = ghost >> 5, ghost & 31
    place_of = jnp.where(
        block == 2, two, jnp.where(block == 1, 1 - two, jnp.where(block == 3, three, 5 - three)))
    nb_out[...] = jnp.where((ghost >= 0) & (ghost < LN), LN + place_of * 32 + slot, nb[...])


def lift_kernel(lift, rotate, s_ref, fine_ref, se_ref, nb_ref, fp_ref, l2_out, lr2_out, order_out,
                spot_out, pack_out, slot_spot, slot_fine, slot_flux, rows):
    is_fine = jnp.broadcast_to(fine_ref[...], (LN, LN))
    down = lax.broadcasted_iota(jnp.int32, (LN, LN), 0)
    across = lanes((LN, LN))
    ahead = (down < across).astype(F32).astype(BF16)
    spot = dot(is_fine.astype(F32).astype(BF16), ahead)
    own_spot = jnp.transpose(spot).astype(jnp.int32)
    own_fine = jnp.transpose(is_fine.astype(F32)) > 0.5
    chosen = own_fine & (own_spot == across % (LN // 2))
    order = dot(across.astype(F32).astype(BF16), chosen.astype(F32).astype(BF16)).astype(jnp.int32)
    order_out[...] = order[0:8]
    low = jnp.minimum(spot.astype(jnp.int32), LN // 2 - 1)
    spot_out[0] = low[0:8]
    spot_out[1] = low[0:8] + LN // 2
    order = order[0:8]
    elem = jnp.broadcast_to(se_ref[...], (8, LN))
    slot_spot[0] = pick(low[0:8], elem)
    slot_spot[1] = slot_spot[0] + LN // 2
    slot_fine[...] = pick(jnp.broadcast_to(fine_ref[...], (8, LN)), elem)
    target = face = jnp.zeros((LN, LN), F32)
    for f in range(4):
        named = jnp.transpose(jnp.broadcast_to(nb_ref[f:f + 1, :], (LN, LN)).astype(F32))
        hit = (named == (across + LN).astype(F32)).astype(F32).astype(BF16)
        target = target + dot(across.astype(F32).astype(BF16), hit)
        face = face + f * dot(jnp.ones((LN, LN), BF16), hit)
    target = target[0:8].astype(jnp.int32)
    face = face[0:1].astype(jnp.int32)
    for q in range(NQ):
        for p in range(NQ):
            got = pick(jnp.concatenate([fp_ref[q, p], jnp.zeros((4, LN), F32)], axis=0), target)
            slot_flux[q, p:p + 1, :] = chosen_face(face, lambda f: got[f:f + 1])
    for q in range(NQ):
        for p in range(q + 1):
            got = pick(jnp.concatenate([s_ref[q, p], jnp.zeros((5, LN), F32)], axis=0), order)
            rows[q, p] = got
            rows[p, q] = got
    left = lanes((3, LN)) < LN // 2

    def entry(q, p):
        return rows[q, p, 0:3] if q < NQ and p < NQ else jnp.zeros((3, LN), F32)

    for j in range(PAIRS):
        for i in range(PAIRS):
            a, b = 2 * j, 2 * i
            pack_out[j, b] = jnp.where(left, entry(a, b), entry(a + 1, b + 1))
            pack_out[j, b + 1] = jnp.where(left, entry(a, b + 1), entry(a + 1, b))
    gap = jnp.zeros((FR - lift.shape[0], NB), F32)
    own, turned = [], [[] for _ in range(3)]
    turns = [jnp.transpose(rotate[k]) for k in range(3)]
    for f in range(4):
        flipped = lift[:, f, :]
        own += [flipped, gap]
        for k in range(3):
            turned[k] += [exact(turns[k], flipped), gap]
    l2_out[...] = two_rows(jnp.transpose(jnp.concatenate(own, axis=0)))
    lr2_out[...] = two_rows(jnp.transpose(jnp.concatenate(turned[0] + turned[1] + turned[2], axis=0)))


def coarse_kernel(series, s_ref, w2, p2, fm_ref, l2, after, u_out, full, t_full):
    del after
    for q in range(NQ):
        full[q] = weigh(series, 1.0, 0.0, q)
    traces(full, p2[...], t_full)
    rows = operator(full, s_ref, w2[...])
    for q in range(NQ):
        u_out[q] = series[0, q] + rows[q] - own_term(fm_ref, t_full, l2[...], q)


def local_kernel(sub, *refs):
    (q_ref, s_ref, w2, p2, fm_ref, l2, fp_ref, lr2, nb_ref, nf_ref, or_ref, series, se, sf, fine_ref,
     spot_ref) = refs[:16]
    if sub == 0:
        pred, t_ref = refs[16:18]
        rest = refs[18:]
    else:
        sums, piece = refs[16:18]
        pred, t_ref = refs[-2:]
        rest = refs[18:-2]
        fine = fine_ref[...] == 1
        for q in range(NQ):
            spot = jnp.broadcast_to(spot_ref[q % 2, 0:1, :], (NB, LN))
            pred[q] = jnp.where(fine, pick(sums[q // 2], spot), piece[q])
        traces(pred, p2[...], t_ref)
    u_out, near_out, *coming, n_ref = rest
    rows = operator(pred, s_ref, w2[...])
    for q in range(NQ):
        u_out[q] = q_ref[q] + rows[q] - own_term(fm_ref, t_ref, l2[...], q)
    local_pick(t_ref, nb_ref, nf_ref, n_ref)
    masks = orient_masks(or_ref)
    for q in range(NQ):
        near_out[q] = turned_lift(lr2[...], masks, flux_rows(fp_ref, q, n_ref))
    if coming:
        piece_out, slots_out = coming
        elem = jnp.broadcast_to(se[...], (NB, LN))
        face = jnp.broadcast_to(sf[...], (FR, LN))
        for q in range(NQ):
            values = weigh(series, (sub + 2) / RATE, (sub + 1) / RATE, q)
            piece_out[q] = values
            table = times(p2[...], pick(values, elem), FA)
            slots_out[q] = chosen_face(face, lambda f: table[f * FR:(f + 1) * FR])


def ghost_terms(refs):
    (g3, g2, g1, g0, flux, lr2, nb_ref, or_ref) = refs
    table = unpack((g0, g1, g2, g3))
    masks = orient_masks(or_ref)
    for q in range(NQ):
        total = flux[q, 0:1, :] * table[:FR]
        for p in range(1, NQ):
            total = total + flux[q, p:p + 1, :] * table[p * FR:(p + 1) * FR]
        yield q, turned_lift(lr2[...], masks, ghost_rows(total, nb_ref))


def last_kernel(*refs):
    u_ref, near, acc, uc_ref, coh, fine_ref, out, work = refs[8:]
    fine = fine_ref[...] == 1
    for q, term in ghost_terms(refs[:8]):
        work[q] = jnp.where(fine, u_ref[q], uc_ref[q] - acc[q]) - near[q] - term
    after = plastic(work, coh[...])
    for q in range(NQ):
        out[q] = after[q]


def join_kernel(first, *refs):
    (u_ref, near, acc, coh, fine_ref, q_ref, pack_ref, w2, p2, slots, sf, order_ref, spot_ref,
     slot_fine, q_out, acc_out, sums, m0, m1, m2, m3, work, series, t_ref) = refs[8:]
    fine = fine_ref[...] == 1
    for q, term in ghost_terms(refs[:8]):
        term = near[q] + term
        work[q] = u_ref[q] - term
        acc_out[q] = term if first else acc[q] + term
    after = plastic(work, coh[...])
    for q in range(NQ):
        q_out[q] = jnp.where(fine, after[q], q_ref[q])
    order = jnp.broadcast_to(order_ref[0:1, :], (NB, LN))
    left = lanes((NB, LN)) < LN // 2
    for j in range(PAIRS):
        rows = pick(q_out[2 * j], order)
        other = pick(q_out[2 * j + 1], order) if 2 * j + 1 < NQ else jnp.zeros((NB, LN), F32)
        rows = jnp.where(left, rows, other)
        both_ways(series.at[0], j, rows)
        sums[j] = rows * (1.0 / RATE)
    for k in range(ORDER - 1):
        weight = (1.0 / RATE) ** (k + 2) / math.factorial(k + 2)
        rows = packed_operator(series.at[k % 2], pack_ref, w2[...])
        for j in range(PAIRS):
            if k < ORDER - 2:
                both_ways(series.at[(k + 1) % 2], j, rows[j])
            sums[j] += weight * rows[j]
    for j in range(PAIRS):
        t_ref[j] = times(p2[...], sums[j], FA)
    send_packed(t_ref, slots, spot_ref, slot_fine, sf, (m0, m1, m2, m3))


BIG = (NQ, NB, LN)
TAB = (NQ, FA, LN)
MSG = (PK, LN)


def call(kernel, name, outs, scratch, args, size=4, space=pltpu.VMEM, limit=24):
    return pl.pallas_call(
        kernel,
        name=name,
        out_shape=[jax.ShapeDtypeStruct(s, d) for s, d in outs],
        in_specs=[pl.BlockSpec(memory_space=space)] * len(args),
        out_specs=[pl.BlockSpec(memory_space=pltpu.VMEM)] * len(outs),
        scratch_shapes=[pltpu.VMEM(*x) if isinstance(x, tuple) else x for x in scratch],
        compiler_params=pltpu.CompilerParams(vmem_limit_bytes=limit << 20),
        cost_estimate=pl.CostEstimate(flops=50_000_000, bytes_accessed=size << 20, transcendentals=0),
    )(*args)


def partners(devices):
    def pairing(step, start, ends):
        pairs = []
        for i in range(devices):
            j = i - start
            t = start + (j ^ step) if j >= 0 else -1
            if t < start or t >= devices:
                t = ends(i)
            pairs.append((i, t))
        return pairs
    return (
        pairing(1, 0, lambda i: i),
        pairing(1, 1, lambda i: devices - 1 - i),
        pairing(2, 0, lambda i: i),
        pairing(2, 2, lambda i: i ^ 1),
    )


def shards(dofs, star, flux_minus, flux_plus, cohesion, stiff, face_proj, lift, rotate, cluster,
           neighbor, neigh_face, orient, send_elem, send_face):
    devices = lax.axis_size("dom")
    pairings = partners(devices)

    def exchange(messages):
        got = [None] * 4
        for k in (2, 3, 1, 0):
            got[k] = lax.ppermute(messages[k], "dom", pairings[k])
        return got

    i32 = jnp.int32
    args = [
        jnp.transpose(dofs, (1, 0, 2)), jnp.transpose(star, (1, 2, 0, 3)),
        jnp.transpose(flux_minus, (1, 2, 0, 3)), jnp.transpose(flux_plus, (1, 2, 0, 3)),
        cohesion.reshape(1, LN), stiff, jnp.transpose(face_proj, (1, 0, 2)),
        jnp.transpose(lift, (2, 0, 1)), rotate, cluster.reshape(1, LN), neighbor, neigh_face,
        orient, send_elem, send_face]
    scratch = [pltpu.VMEM(args[n].shape, args[n].dtype) for n in (1, 5, 6, 13, 14, 10)]
    outs = call(
        first_kernel, "first",
        [((NQ, NQ, 3, LN), F32), ((2 * NB, 3 * NB), BF16), ((2 * FA, NB), BF16),
         ((ORDER,) + BIG, F32), (BIG, F32), (TAB, F32)] + [(MSG, F32)] * 4
        + [((1, LN), i32), ((1, LN), i32), ((4, LN), i32), (args[2].shape, F32),
           (args[3].shape, F32), ((4, LN), i32), ((4, LN), i32), ((1, LN), F32), ((1, LN), i32),
           (args[7].shape, F32), (args[8].shape, F32)],
        scratch + [pltpu.SemaphoreType.DMA((15,))],
        [pltpu.with_memory_space_constraint(a, pltpu.HBM) for a in args], space=pltpu.HBM)
    s_mat, w2, p2, series, pred, table = outs[:6]
    got = exchange(outs[6:10])
    se, sf, nb, fm, fp, nf, turn_code, coh, fine, lift, rotate = outs[10:]
    l2, lr2, order, spot, packed, slot_spot, slot_fine, slot_flux = call(
        lift_kernel, "lifts",
        [((2 * NB, FA), BF16), ((2 * NB, 3 * FA), BF16), ((8, LN), i32), ((2, 8, LN), i32),
         ((PAIRS, 2 * PAIRS, 3, LN), F32), ((2, 8, LN), i32), ((8, LN), i32), ((NQ, NQ, LN), F32)],
        [((NQ, NQ, 8, LN), F32)],
        [lift, rotate, s_mat, fine, se, nb, fp])
    acc = sums = piece = None
    state = series[0]
    half = ((PAIRS, NB, LN), F32)
    for sub in range(RATE):
        last = sub == RATE - 1
        u, near, *coming = call(
            functools.partial(local_kernel, sub), "local",
            [(BIG, F32), (BIG, F32)] + ([] if last else [(BIG, F32), ((NQ, FR, LN), F32)]),
            [(TAB, F32)] + ([(BIG, F32), (TAB, F32)] if sub else []),
            [state, s_mat, w2, p2, fm, l2, fp, lr2, nb, nf, turn_code, series, se, sf, fine, spot]
            + ([sums, piece] if sub else [pred, table]), 8)
        if sub == 1:
            coarse = call(
                coarse_kernel, "coarse_own", [(BIG, F32)], [(BIG, F32), (TAB, F32)],
                [series, s_mat, w2, p2, fm, l2, outs[3]], 8)[0]
        common = [got[3], got[2], got[1], got[0], slot_flux, lr2, nb, turn_code, u, near]
        if last:
            out = call(
                last_kernel, "last", [(BIG, F32)], [(BIG, F32)],
                common + [acc, coarse, coh, fine])[0]
            return jnp.transpose(out, (1, 0, 2))
        piece, slots = coming
        outs = call(
            functools.partial(join_kernel, acc is None), "join",
            [(BIG, F32), (BIG, F32), half] + [(MSG, F32)] * 4,
            [(BIG, F32), ((2, 2 * PAIRS, NB, LN), F32), ((PAIRS, FA, LN), F32)],
            common + [near if acc is None else acc, coh, fine, state, packed, w2, p2, slots, sf,
                      order, slot_spot, slot_fine])
        state, acc, sums = outs[:3]
        got = exchange(outs[3:])


def solution(mesh):
    placed = (
        P(None, None, "dom"),
        P(None, None, None, "dom"),
        P(None, None, None, "dom"),
        P(None, None, None, "dom"),
        P("dom"),
        P(),
        P(),
        P(),
        P(),
        P("dom"),
        P(None, "dom"),
        P(None, "dom"),
        P(None, "dom"),
        P(None, "dom"),
        P(None, "dom"),
    )
    return jax.shard_map(
        shards, mesh=mesh, in_specs=placed, out_specs=P(None, None, "dom"), check_vma=False)
```
